256 devices in a mesh: dp: 4 (over x), expert: 4 (over y), tensor: 16 (over z, core).
Axes of the slice: x: 4, y: 4, z: 8, core: 2. Of those that a mesh axis runs over, the one named last changes fastest.
Arguments:
- tokens: bfloat16 [2048, 4096], P('expert', 'dp'), may hold values from -6 to 6
- labels: int32 [2048, 1], P('expert'), may hold values from 0 to 7; in each aligned block of 512 rows (0 to 511, 512 to 1023, ...) at most 96 rows name the same one
- grad_out: bfloat16 [2048, 4096], P('expert', 'dp'), may hold values from -1.5 to 1.5
- w_gate: bfloat16 [8, 4096, 7168], P('expert', 'dp', 'tensor'), may hold values from -0.09375 to 0.09375
- w_up: bfloat16 [8, 4096, 7168], P('expert', 'dp', 'tensor'), may hold values from -0.09375 to 0.09375
- w_down: bfloat16 [8, 7168, 4096], P('expert', 'tensor', 'dp'), may hold values from -0.0625 to 0.0625
Outputs:
- mixed: bfloat16 [2048, 4096], P('expert', 'dp')
- grad_tokens: bfloat16 [2048, 4096], P('expert', 'dp')
- grad_gate: bfloat16 [8, 4096, 7168], P('expert', 'dp', 'tensor')
- grad_up: bfloat16 [8, 4096, 7168], P('expert', 'dp', 'tensor')
- grad_down: bfloat16 [8, 7168, 4096], P('expert', 'tensor', 'dp')
The draws below stay inside these ranges and needn't reach their ends.
Inputs may be any that keep to these rules, and one draw needn't show every extreme that they name: `labels`: in each aligned block of 512 rows (the rows of one index of expert) no domain appears more than 96 times; some domain appears exactly 96 times in some block. Every domain appears somewhere.
All inputs are finite; a program needn't handle non-finite values.
Results may differ from the reference program's by a relative error of at most 0.005.
Values may be sent and summed in bfloat16 or wider, within the bound.
A program may use at most 128 MiB of HBM per device.

```python
import math
import jax
import jax.numpy as jnp
import numpy as np
from jax import lax

D = 4096
FF = 7168
TOK_DEV = 512
MOST = 96
EXPERTS = 8
TOKENS = 2048


def levels(stream_key, extent, split, low, high):
    def one(dim, blocks):
        heights = jax.random.uniform(jax.random.fold_in(jax.random.fold_in(stream_key, 6), dim), (blocks,), jnp.float32, low / len(split), high / len(split))
        return jnp.repeat(jnp.exp(heights), extent[dim] // blocks).reshape((-1,) + (1,) * (len(extent) - dim - 1))

    loudness = one(*split[0])
    for cut in split[1:]:
        loudness = loudness * one(*cut)
    return loudness


def deal_out(key, own, number, rows, amount, top, most, lean):
    ranking = jax.random.permutation(key, amount)
    heavy_load, common = portions_of(amount, rows * top, most, lean, True), portions_of(amount, rows * top, most, lean, False)
    places = jnp.arange(amount)

    def named(sizes, rotation):
        used = int((sizes > 0).sum())
        fixed = max(1, used // 4)
        moved = fixed + (places - fixed + rotation * (used - fixed)) % max(1, amount - fixed)
        return jnp.zeros((amount,), jnp.int32).at[ranking[jnp.where(places < fixed, places, moved)]].set(jnp.asarray(sizes, jnp.int32))

    sizes = jnp.where(number % 4 == 0, named(heavy_load, number // 4), named(common, number - number // 4 - 1))
    mixed = jax.random.permutation(jax.random.fold_in(own, 3), amount)
    giver, receiver = mixed[0:amount // 2 * 2:2], mixed[1:amount // 2 * 2:2]
    slack = jnp.minimum(sizes[giver] - 1, most - sizes[receiver]) // 2
    slack = jnp.where((giver == ranking[0]) | (receiver == ranking[0]) | (sizes[receiver] == 0), 0, jnp.maximum(slack, 0))
    moved = jax.random.randint(jax.random.fold_in(own, 4), (amount // 2,), 0, 1 << 20) % (slack + 1)
    sizes = sizes.at[giver].add(-moved).at[receiver].add(moved)
    items = jnp.searchsorted(jnp.cumsum(sizes), jnp.arange(rows * top), side="right").astype(jnp.int32)
    grid = items.reshape(top, rows).T
    grid = grid[jax.random.permutation(jax.random.fold_in(own, 1), rows)]
    rotation = jax.random.randint(jax.random.fold_in(own, 2), (rows, 1), 0, top)
    return jnp.take_along_axis(grid, (jnp.arange(top)[None, :] + rotation) % top, axis=1)


def portions_of(count, total, reach, lean, full):
    loads = [(1 << 20) // math.isqrt(rank ** lean) + 1 for rank in range(1, count + 1)]
    largest = reach if full else min(reach, max(-(-total // count), total * loads[0] // sum(loads)))
    least = 1 if total - largest >= count - 1 else 0
    counts, spare = [largest] + [least] * (count - 1), total - largest - least * (count - 1)
    while spare > 0:
        movable = [i for i in range(1, count) if counts[i] < largest] or [i for i in range(1, count) if counts[i] < reach]
        pool, budget = sum([loads[i] for i in movable]), spare
        for i in movable:
            addition = min(reach - counts[i], max(1, budget * loads[i] // pool), spare)
            counts[i] = counts[i] + addition
            spare = spare - addition
    return np.array(counts)


def scatter_about(stream_key, shape, width, limit, cuts=(), kind=jnp.bfloat16):
    level = levels(stream_key, shape, cuts, -0.22, 0.18) if cuts else 1.0
    result = jax.random.normal(stream_key, shape, jnp.float32) * width * level
    return jnp.minimum(jnp.maximum(result, -limit), limit).astype(kind)


def setup_inputs(seed: int = 0) -> dict:
    arg_keys = jax.random.split(jax.random.key(seed), 7)
    tokens = scatter_about(arg_keys[0], (TOKENS, D), 1.0, 6.0, ((0, 4), (1, 4)))
    labels_keys = jax.random.split(jax.random.fold_in(arg_keys[1], 1), TOKENS // TOK_DEV)
    labels_turns = jax.random.permutation(jax.random.fold_in(arg_keys[1], 3), TOKENS // TOK_DEV)
    labels = jax.vmap(lambda own, number: deal_out(jax.random.fold_in(arg_keys[1], 2), own, number, TOK_DEV, EXPERTS, 1, MOST, 2))(labels_keys, labels_turns).reshape((TOKENS, 1))
    grad_out = scatter_about(arg_keys[2], (TOKENS, D), 0.25, 1.5, ((0, 4), (1, 4)))
    w_gate = scatter_about(arg_keys[3], (EXPERTS, D, FF), D ** -0.5, 0.09375, ((0, 4), (1, 4), (2, 16)))
    w_up = scatter_about(arg_keys[4], (EXPERTS, D, FF), D ** -0.5, 0.09375, ((0, 4), (1, 4), (2, 16)))
    w_down = scatter_about(arg_keys[5], (EXPERTS, FF, D), FF ** -0.5, 0.0625, ((0, 4), (1, 16), (2, 4)))
    return dict(tokens=tokens, labels=labels, grad_out=grad_out, w_gate=w_gate, w_up=w_up, w_down=w_down)


def reference(tokens, labels, grad_out, w_gate, w_up, w_down):
    domain = labels[:, 0]
    capacity = MOST * (TOKENS // TOK_DEV)

    def per_expert(expert):
        hits = domain == expert
        row_index = jnp.nonzero(hits, size=capacity, fill_value=0)[0].astype(jnp.int32)
        tally = jnp.sum(hits.astype(jnp.int32))
        is_valid = (jnp.arange(capacity, dtype=jnp.int32) < tally).astype(jnp.bfloat16)
        expert_in = tokens[row_index] * is_valid[:, None]
        expert_grad = grad_out[row_index] * is_valid[:, None]
        gate_w = w_gate[expert]
        up_w = w_up[expert]
        down_w = w_down[expert]
        gate_sum = jnp.dot(expert_in, gate_w, preferred_element_type=jnp.float32)
        up_sum = jnp.dot(expert_in, up_w, preferred_element_type=jnp.float32)
        back_sum = jnp.dot(expert_grad, down_w.T, preferred_element_type=jnp.float32)
        sigmoid_gate = jax.nn.sigmoid(gate_sum)
        active = gate_sum * sigmoid_gate
        hidden = (active * up_sum).astype(jnp.bfloat16)
        d_gate = (back_sum * up_sum * (sigmoid_gate * (1.0 + gate_sum * (1.0 - sigmoid_gate)))).astype(jnp.bfloat16)
        d_up = (back_sum * active).astype(jnp.bfloat16)
        out_rows = jnp.dot(hidden, down_w, preferred_element_type=jnp.float32)
        in_grad = jnp.dot(d_gate, gate_w.T, preferred_element_type=jnp.float32) + jnp.dot(d_up, up_w.T, preferred_element_type=jnp.float32)
        grad_g = jnp.dot(expert_in.T, d_gate, preferred_element_type=jnp.float32).astype(jnp.bfloat16)
        grad_u = jnp.dot(expert_in.T, d_up, preferred_element_type=jnp.float32).astype(jnp.bfloat16)
        grad_d = jnp.dot(hidden.T, expert_grad, preferred_element_type=jnp.float32).astype(jnp.bfloat16)
        keep = is_valid.astype(jnp.float32)[:, None]
        return row_index, out_rows * keep, in_grad * keep, grad_g, grad_u, grad_d

    row_index, out_rows, in_grad, grad_gate, grad_up, grad_down = lax.map(per_expert, jnp.arange(EXPERTS, dtype=jnp.int32))
    flat_index = row_index.reshape(-1)
    mixed = jnp.zeros((TOKENS, D), jnp.float32).at[flat_index].add(out_rows.reshape(-1, D))
    grad_tokens = jnp.zeros((TOKENS, D), jnp.float32).at[flat_index].add(in_grad.reshape(-1, D))
    return mixed.astype(jnp.bfloat16), grad_tokens.astype(jnp.bfloat16), grad_gate, grad_up, grad_down
```

```python
import jax
import jax.numpy as jnp
from jax import lax
from jax.experimental import pallas as pl
from jax.experimental.pallas import tpu as pltpu
from jax.sharding import PartitionSpec as P

MOST = 96
NX, NY, NZ = 4, 4, 8
TOK = 512
FEAT = 1024
HID = 448
SLICE = HID // NX
ROWS = NY * MOST
COL = FEAT // NZ
BF = jnp.bfloat16
F32 = jnp.float32
MESH = pl.DeviceIdType.MESH


def nt(a, b):
    return lax.dot_general(a, b, (((1,), (1,)), ((), ())), preferred_element_type=F32)


def tn(a, b):
    return lax.dot_general(a, b, (((0,), (0,)), ((), ())), preferred_element_type=F32)


def nn(a, b):
    return jnp.dot(a, b, preferred_element_type=F32)


class RingGather:
    def __init__(self, region, z, right, left, sibling, sems, plus, minus):
        self.region, self.z = region, z
        self.dev = (right, left)
        self.sibling = sibling
        self.zs, self.zr, self.ss, self.sr = sems
        self.count = (plus, minus)
        self.sent = []
        self.hops = ({}, {})
        self.twins = []

    def chunk(self, way, hop):
        return lax.rem(self.z + (NZ - hop if way == 0 else hop), NZ)

    def send(self, way, hop):
        part = self.region(self.chunk(way, hop))
        copy = pltpu.make_async_remote_copy(
            part, part, self.zs.at[way, hop], self.zr.at[way, hop], self.dev[way], MESH
        )
        copy.start()
        self.hops[way][hop] = copy

    def twin(self, chunk, number):
        part = self.region(chunk)
        copy = pltpu.make_async_remote_copy(
            part, part, self.ss.at[number], self.sr.at[number], self.sibling, MESH
        )
        copy.start()
        self.twins.append(copy)

    def start(self):
        for way in (0, 1):
            self.send(way, 0)
        self.twin(self.z, 0)

    def step(self, hop):
        for way in (0, 1):
            if hop < self.count[way]:
                self.hops[way][hop].wait_recv()
                if hop + 1 < self.count[way]:
                    self.send(way, hop + 1)
                self.twin(self.chunk(way, hop + 1), 1 + hop + (self.count[0] if way else 0))

    def finish(self):
        for copy in self.twins:
            copy.wait_recv()

    def drain(self):
        for way in (0, 1):
            for copy in self.hops[way].values():
                copy.wait_send()
        for copy in self.twins:
            copy.wait_send()


def kernel(
    lab_ref,
    tok_hbm,
    go_hbm,
    wg_hbm,
    wu_hbm,
    wd_hbm,
    mix_hbm,
    gt_hbm,
    gg_hbm,
    gu_hbm,
    gd_hbm,
    src,
    w,
    slots,
    outgo,
    x,
    part,
    part16,
    via,
    joined,
    got,
    acts,
    keep,
    twin_out,
    twin_in,
    rows_out,
    ring_out,
    ring_in,
    final,
    home,
    out,
    wgrad,
    load_sem,
    store_sem,
    y_s,
    y_r,
    az_s,
    az_r,
    as_s,
    as_r,
    b_s,
    b_r,
    c_s,
    c_r,
    t_s,
    t_r,
    r_s,
    r_r,
    h_s,
    h_r,
    gz_s,
    gz_r,
    gs_s,
    gs_r,
):
    d = lax.axis_index("dp")
    g = lax.axis_index("expert")
    t = lax.axis_index("tensor")
    z = lax.div(t, 2)
    c = lax.rem(t, 2)
    other = 1 - c
    right = lax.rem(d + 1, NX)
    left = lax.rem(d + NX - 1, NX)
    far = lax.rem(d + 2, NX)
    z_up = {"tensor": lax.rem(z + 1, NZ) * 2 + c}
    z_down = {"tensor": lax.rem(z + NZ - 1, NZ) * 2 + c}
    sibling = {"tensor": z * 2 + other}
    x_dev = ({"dp": right}, {"dp": left})
    group = [lax.rem(g + o, NY) for o in range(NY)]

    def cols(q):
        return pl.ds(pl.multiple_of(q * COL, COL), COL)

    def rows(q):
        return pl.ds(pl.multiple_of(q * SLICE, 16), SLICE)

    barrier = pltpu.get_barrier_semaphore()
    greet = [z_up, z_down, sibling, x_dev[0], x_dev[1]]
    for o in range(1, NY):
        greet.append({"expert": group[o]})
        greet.append({"expert": group[o], "tensor": z * 2 + other})
    for peer in greet:
        pl.semaphore_signal(barrier, inc=1, device_id=peer, device_id_type=MESH)

    loads = [
        pltpu.make_async_copy(tok_hbm, src.at[0], load_sem.at[0]),
        pltpu.make_async_copy(go_hbm, src.at[1], load_sem.at[1]),
        pltpu.make_async_copy(wg_hbm, w.at[0], load_sem.at[2]),
        pltpu.make_async_copy(wu_hbm, w.at[1], load_sem.at[3]),
        pltpu.make_async_copy(wd_hbm, w.at[2], load_sem.at[4]),
    ]
    for copy in loads:
        copy.start()

    lab = lab_ref[...]
    onehot = jnp.where(
        lax.broadcasted_iota(jnp.int32, (8, TOK), 0) == lab, 1.0, 0.0
    )
    earlier = jnp.where(
        lax.broadcasted_iota(jnp.int32, (TOK, TOK), 0)
        < lax.broadcasted_iota(jnp.int32, (TOK, TOK), 1),
        1.0,
        0.0,
    ).astype(BF)
    rank = jnp.sum(nn(onehot.astype(BF), earlier) * onehot, axis=0, keepdims=True)
    relative = ((lab >> 1) - g + NY) & (NY - 1)
    place = relative.astype(F32) * float(MOST) + rank
    spot = lax.broadcasted_iota(jnp.int32, (ROWS, TOK), 0).astype(F32)
    for j in range(2):
        mine = jnp.where((lab & 1) == j, place, -1.0)
        slots[j] = jnp.where(spot == mine, 1.0, 0.0).astype(BF)

    y_copies = [[], []]

    def dispatch(k):
        loads[k].wait()
        picked = nn(slots[c, pl.ds(MOST, ROWS - MOST)], src[k, :, cols(z)])
        outgo[k] = picked.astype(BF)
        if k == 0:
            pl.semaphore_wait(barrier, len(greet))
        for o in (1, 3, 2):
            back = NY - o
            copy = pltpu.make_async_remote_copy(
                outgo.at[k, pl.ds((o - 1) * MOST, MOST)],
                x.at[k, c, pl.ds(back * MOST, MOST), cols(z)],
                y_s.at[k, o - 1],
                y_r.at[k, o - 1],
                {"expert": group[o]},
                MESH,
            )
            copy.start()
            y_copies[k].append(copy)

    def own_rows(k):
        for j in range(2):
            x[k, j, pl.ds(0, MOST)] = nn(slots[j, pl.ds(0, MOST)], src[k]).astype(BF)

    gathers = [
        RingGather(
            lambda q, k=k: x.at[k, c, pl.ds(MOST, ROWS - MOST), cols(q)],
            z,
            z_up,
            z_down,
            sibling,
            (az_s.at[k], az_r.at[k], as_s.at[k], as_r.at[k]),
            *((4, 3) if k == 0 else (3, 4)),
        )
        for k in range(2)
    ]

    def begin(k):
        for copy in y_copies[k]:
            copy.wait_recv()
        gathers[k].start()

    b_copies = {}

    def push(table, key, source, target, send, recv, way):
        copy = pltpu.make_async_remote_copy(source, target, send, recv, x_dev[way], MESH)
        copy.start()
        table[key] = copy

    def partial(k):
        inputs = 1 if k == 2 else 0

        @pl.loop(0, 2)
        def _(j):
            value = nt(w[k, j], x[inputs, j])
            part[k, j] = value
            part16[k, j] = value.astype(BF)

        for way, (near, j) in enumerate(((right, 0), (left, 1))):
            push(
                b_copies, (k, way, 0), part16.at[k, j, rows(far)], via.at[k, way],
                b_s.at[k, way, 0], b_r.at[k, way, 0], way,
            )
        for way, (near, j) in enumerate(((right, 0), (left, 1))):
            push(
                b_copies, (k, way, 1), part16.at[k, 1 - j, rows(near)], got.at[k, way, 1 - j],
                b_s.at[k, way, 1], b_r.at[k, way, 1], way,
            )

    def join(k):
        for way, (near, j) in enumerate(((right, 0), (left, 1))):
            b_copies[k, way, 0].wait_recv()
            joined[k, way] = (part[k, j, rows(near)] + via[k, way].astype(F32)).astype(BF)
            push(
                b_copies, (k, way, 2), joined.at[k, way], got.at[k, way, j],
                b_s.at[k, way, 2], b_r.at[k, way, 2], way,
            )

    def arrived(k):
        for way in (0, 1):
            for piece in (1, 2):
                b_copies[k, way, piece].wait_recv()

    def total(k, j):
        return part[k, j, rows(d)] + got[k, 0, j].astype(F32) + got[k, 1, j].astype(F32)

    c_copies = {}

    def share(n):
        for piece in (0, 1):
            for way in (0, 1):
                j = piece ^ way
                block = acts.at[n, j, rows(d)]
                push(
                    c_copies, (n, way, piece), block, block,
                    c_s.at[n, way, piece], c_r.at[n, way, piece], way,
                )

    def relay(n):
        for way, origin in enumerate((left, right)):
            c_copies[n, way, 0].wait_recv()
            block = acts.at[n, way, rows(origin)]
            push(
                c_copies, (n, way, 2), block, block,
                c_s.at[n, way, 2], c_r.at[n, way, 2], way,
            )

    def shared(n):
        for way in (0, 1):
            for piece in (1, 2):
                c_copies[n, way, piece].wait_recv()

    def forward_acts():
        for j in range(2):
            gate = total(0, j)
            up = total(1, j)
            sig = jax.nn.sigmoid(gate)
            active = gate * sig
            acts[0, j, rows(d)] = (active * up).astype(BF)
            keep[0, j] = up * (sig * (1.0 + gate * (1.0 - sig)))
            keep[1, j] = active
        share(0)

    def backward_acts():
        for j in range(2):
            back = total(2, j)
            acts[1, j, rows(d)] = (back * keep[0, j]).astype(BF)
            acts[2, j, rows(d)] = (back * keep[1, j]).astype(BF)
        share(1)
        share(2)

    def rows_of(kd, j):
        if kd == 0:
            return tn(acts[0, j], w[2, j])
        return tn(acts[1, j], w[0, j]) + tn(acts[2, j], w[1, j])

    t_copies = []

    def expand(kd):
        twin_out[kd] = rows_of(kd, other)
        copy = pltpu.make_async_remote_copy(
            twin_out.at[kd], twin_in.at[kd], t_s.at[kd], t_r.at[kd], sibling, MESH
        )
        copy.start()
        t_copies.append(copy)
        rows_out[kd] = rows_of(kd, c)

    ring = {}
    counts = ((4, 3), (3, 4))

    def chunk_sum(kd, q):
        return rows_out[kd, :, cols(q)] + twin_in[kd, :, cols(q)]

    def reduce_step(kd, i):
        if i == 0:
            t_copies[kd].wait_recv()
        for way in (0, 1):
            n = counts[kd][way]
            if i >= n:
                continue
            ahead = n - i
            q = lax.rem(z + (ahead if way == 0 else NZ - ahead), NZ)
            value = chunk_sum(kd, q)
            if i > 0:
                ring[kd, way, i - 1].wait_recv()
                value = value + ring_in[kd, way, i - 1].astype(F32)
            ring_out[kd, way, i] = value.astype(BF)
            copy = pltpu.make_async_remote_copy(
                ring_out.at[kd, way, i], ring_in.at[kd, way, i],
                r_s.at[kd, way, i], r_r.at[kd, way, i],
                (z_up, z_down)[way], MESH,
            )
            copy.start()
            ring[kd, way, i] = copy

    h_copies = [[], []]

    def go_home(kd):
        value = chunk_sum(kd, z)
        for way in (0, 1):
            last = counts[kd][way] - 1
            ring[kd, way, last].wait_recv()
            value = value + ring_in[kd, way, last].astype(F32)
        value = value.astype(BF)
        final[kd] = value
        home[kd, c, pl.ds(0, MOST)] = value[:MOST]
        for o in (2, 1, 3, 0):
            back = (NY - o) % NY
            for same in (0, 1):
                if o == 0 and same == 0:
                    continue
                core = c if same == 0 else other
                copy = pltpu.make_async_remote_copy(
                    final.at[kd, pl.ds(o * MOST, MOST)],
                    home.at[kd, c, pl.ds(back * MOST, MOST)],
                    h_s.at[kd, same, o],
                    h_r.at[kd, same, o],
                    {"expert": group[o], "tensor": z * 2 + core},
                    MESH,
                )
                copy.start()
                h_copies[kd].append(copy)

    half = pl.ds(pl.multiple_of(c * (TOK // 2), TOK // 2), TOK // 2)
    outs = [
        RingGather(
            lambda q, kd=kd: out.at[kd, half, cols(q)],
            z,
            z_up,
            z_down,
            sibling,
            (gz_s.at[kd], gz_r.at[kd], gs_s.at[kd], gs_r.at[kd]),
            *counts[kd],
        )
        for kd in range(2)
    ]

    def settle(kd):
        for copy in h_copies[kd]:
            copy.wait_recv()
        value = tn(slots[0, :, half], home[kd, 0]) + tn(slots[1, :, half], home[kd, 1])
        out[kd, half, cols(z)] = value.astype(BF)
        outs[kd].start()

    stores = []

    def store(source, target, number):
        copy = pltpu.make_async_copy(source, target, store_sem.at[number])
        copy.start()
        stores.append(copy)

    def weight_grad(n, k, target):
        @pl.loop(0, 2)
        def _(j):
            wgrad[n, j] = nn(acts[n, j], x[k, j]).astype(BF)

        store(wgrad.at[n], target, n)

    dispatch(0)
    dispatch(1)
    own_rows(0)
    begin(0)
    own_rows(1)
    gathers[0].step(0)
    begin(1)
    gathers[0].step(1)
    gathers[1].step(0)
    gathers[0].step(2)
    gathers[1].step(1)
    gathers[0].step(3)
    gathers[0].finish()
    loads[2].wait()
    partial(0)
    gathers[1].step(2)
    loads[3].wait()
    partial(1)
    join(0)
    gathers[1].step(3)
    gathers[1].finish()
    join(1)
    loads[4].wait()
    partial(2)
    arrived(0)
    arrived(1)
    forward_acts()
    join(2)
    relay(0)
    arrived(2)
    backward_acts()
    shared(0)
    expand(0)
    reduce_step(0, 0)
    relay(1)
    relay(2)
    reduce_step(0, 1)
    weight_grad(0, 1, gd_hbm)
    reduce_step(0, 2)
    shared(1)
    shared(2)
    reduce_step(0, 3)
    expand(1)
    go_home(0)
    reduce_step(1, 0)
    reduce_step(1, 1)
    settle(0)
    weight_grad(1, 0, gg_hbm)
    reduce_step(1, 2)
    outs[0].step(0)
    reduce_step(1, 3)
    outs[0].step(1)
    go_home(1)
    weight_grad(2, 0, gu_hbm)
    outs[0].step(2)
    settle(1)
    outs[0].step(3)
    outs[1].step(0)
    outs[0].finish()
    store(out.at[0], mix_hbm, 3)
    for hop in (1, 2, 3):
        outs[1].step(hop)
    outs[1].finish()
    store(out.at[1], gt_hbm, 4)

    for ring_gather in gathers + outs:
        ring_gather.drain()
    for copy in y_copies[0] + y_copies[1] + t_copies + h_copies[0] + h_copies[1]:
        copy.wait_send()
    for table in (b_copies, c_copies, ring):
        for copy in table.values():
            copy.wait_send()
    for copy in stores:
        copy.wait()


def body(tokens, labels, grad_out, w_gate, w_up, w_down):
    dma = pltpu.SemaphoreType.DMA
    scratch = [
        pltpu.VMEM((2, TOK, FEAT), BF),
        pltpu.VMEM((3, 2, HID, FEAT), BF),
        pltpu.VMEM((2, ROWS, TOK), BF),
        pltpu.VMEM((2, ROWS - MOST, COL), BF),
        pltpu.VMEM((2, 2, ROWS, FEAT), BF),
        pltpu.VMEM((3, 2, HID, ROWS), F32),
        pltpu.VMEM((3, 2, HID, ROWS), BF),
        pltpu.VMEM((3, 2, SLICE, ROWS), BF),
        pltpu.VMEM((3, 2, SLICE, ROWS), BF),
        pltpu.VMEM((3, 2, 2, SLICE, ROWS), BF),
        pltpu.VMEM((3, 2, HID, ROWS), BF),
        pltpu.VMEM((2, 2, SLICE, ROWS), F32),
        pltpu.VMEM((2, ROWS, FEAT), F32),
        pltpu.VMEM((2, ROWS, FEAT), F32),
        pltpu.VMEM((2, ROWS, FEAT), F32),
        pltpu.VMEM((2, 2, 4, ROWS, COL), BF),
        pltpu.VMEM((2, 2, 4, ROWS, COL), BF),
        pltpu.VMEM((2, ROWS, COL), BF),
        pltpu.VMEM((2, 2, ROWS, COL), BF),
        pltpu.VMEM((2, TOK, FEAT), BF),
        pltpu.VMEM((3, 2, HID, FEAT), BF),
        dma((5,)),
        dma((5,)),
        dma((2, 3)),
        dma((2, 3)),
        dma((2, 2, 4)),
        dma((2, 2, 4)),
        dma((2, 8)),
        dma((2, 8)),
        dma((3, 2, 3)),
        dma((3, 2, 3)),
        dma((3, 2, 3)),
        dma((3, 2, 3)),
        dma((2,)),
        dma((2,)),
        dma((2, 2, 4)),
        dma((2, 2, 4)),
        dma((2, 2, 4)),
        dma((2, 2, 4)),
        dma((2, 2, 4)),
        dma((2, 2, 4)),
        dma((2, 8)),
        dma((2, 8)),
    ]
    anywhere = pl.BlockSpec(memory_space=pl.ANY)
    mixed, grad_tokens, gate_t, up_t, down = pl.pallas_call(
        kernel,
        out_shape=(
            jax.ShapeDtypeStruct((TOK, FEAT), BF),
            jax.ShapeDtypeStruct((TOK, FEAT), BF),
            jax.ShapeDtypeStruct((2, HID, FEAT), BF),
            jax.ShapeDtypeStruct((2, HID, FEAT), BF),
            jax.ShapeDtypeStruct((2, HID, FEAT), BF),
        ),
        in_specs=[pl.BlockSpec(memory_space=pltpu.VMEM)] + [anywhere] * 5,
        out_specs=(anywhere,) * 5,
        scratch_shapes=scratch,
        compiler_params=pltpu.CompilerParams(
            collective_id=0, has_side_effects=True, vmem_limit_bytes=50 * 1024 * 1024
        ),
    )(
        labels.reshape(1, TOK),
        tokens,
        grad_out,
        jnp.swapaxes(w_gate, 1, 2),
        jnp.swapaxes(w_up, 1, 2),
        w_down,
    )
    return mixed, grad_tokens, jnp.swapaxes(gate_t, 1, 2), jnp.swapaxes(up_t, 1, 2), down


def solution(mesh):
    in_specs = (
        P("expert", "dp"),
        P("expert", None),
        P("expert", "dp"),
        P("expert", "dp", "tensor"),
        P("expert", "dp", "tensor"),
        P("expert", "tensor", "dp"),
    )
    out_specs = (
        P("expert", "dp"),
        P("expert", "dp"),
        P("expert", "dp", "tensor"),
        P("expert", "dp", "tensor"),
        P("expert", "tensor", "dp"),
    )
    return jax.shard_map(body, mesh=mesh, in_specs=in_specs, out_specs=out_specs, check_vma=False)
```

```python
import jax
import jax.numpy as jnp
from jax import lax
from jax.experimental import pallas as pl
from jax.experimental.pallas import tpu as pltpu
from jax.sharding import PartitionSpec as P

MOST = 96
NX, NY, NZ = 4, 4, 8
TOK = 512
FEAT = 1024
HID = 448
SLICE = HID // NX
ROWS = NY * MOST
COL = FEAT // NZ
PART = FEAT // 2
SHARE = MOST // 2
HALF = NY * SHARE
BF = jnp.bfloat16
F32 = jnp.float32
MESH = pl.DeviceIdType.MESH


def nt(a, b):
    return lax.dot_general(a, b, (((1,), (1,)), ((), ())), preferred_element_type=F32)


def tn(a, b):
    return lax.dot_general(a, b, (((0,), (0,)), ((), ())), preferred_element_type=F32)


def nn(a, b):
    return jnp.dot(a, b, preferred_element_type=F32)


def take(ref, sem):
    pltpu.make_async_copy(ref, ref, sem).wait()


class RingGather:
    def __init__(self, region, z, right, left, sibling, sems, plus, minus):
        self.region, self.z = region, z
        self.dev = (right, left)
        self.sibling = sibling
        self.zs, self.zr, self.ss, self.sr = sems
        self.count = (plus, minus)

    def chunk(self, way, hop):
        return lax.rem(self.z + (NZ - hop if way == 0 else hop), NZ)

    def number(self, way, hop):
        return hop + (self.count[0] if way else 0)

    def send(self, way, hop):
        part = self.region(self.chunk(way, hop))
        pltpu.make_async_remote_copy(
            part, part, self.zs, self.zr.at[self.number(way, hop)], self.dev[way], MESH
        ).start()

    def twin(self, chunk):
        part = self.region(chunk)
        pltpu.make_async_remote_copy(part, part, self.ss, self.sr, self.sibling, MESH).start()

    def start(self):
        for way in (0, 1):
            self.send(way, 0)
        self.twin(self.z)

    def step(self, hop):
        for way in (0, 1):
            if hop < self.count[way]:
                chunk = self.chunk(way, hop + 1)
                take(self.region(chunk), self.zr.at[self.number(way, hop)])
                if hop + 1 < self.count[way]:
                    self.send(way, hop + 1)
                self.twin(chunk)


def kernel(
    lab_hbm,
    tok_hbm,
    go_hbm,
    wg_hbm,
    wu_hbm,
    wd_hbm,
    out,
    wgrad,
    lab_ref,
    src,
    w,
    slots,
    outgo,
    passing,
    x,
    part,
    part16,
    land,
    joined,
    acts,
    keep,
    twin_in,
    early_in,
    early_out,
    rows_out,
    ring_out,
    ring_in,
    final,
    home,
    load_sem,
    sent,
    y_r,
    z_r,
    w_r,
    v_r,
    b_r,
    c_r,
    f_r,
    t_r,
    e_r,
    r_r,
    h_r,
    gz_r,
    gs_r,
):
    d = lax.axis_index("dp")
    g = lax.axis_index("expert")
    t = lax.axis_index("tensor")
    z = lax.div(t, 2)
    c = lax.rem(t, 2)
    other = 1 - c
    right = lax.rem(d + 1, NX)
    left = lax.rem(d + NX - 1, NX)
    far = lax.rem(d + 2, NX)
    z_up = {"tensor": lax.rem(z + 1, NZ) * 2 + c}
    z_down = {"tensor": lax.rem(z + NZ - 1, NZ) * 2 + c}
    sibling = {"tensor": z * 2 + other}
    x_dev = ({"dp": right}, {"dp": left})
    s_y, s_z, s_w, s_b, s_c, s_t, s_e, s_r, s_h, s_gz, s_gs = [sent.at[i] for i in range(11)]
    group = [lax.rem(g + o, NY) for o in range(NY)]

    def cols(q):
        return pl.ds(pl.multiple_of(q * COL, COL), COL)

    def rows(q):
        return pl.ds(pl.multiple_of(q * SLICE, 16), SLICE)

    barrier = pltpu.get_barrier_semaphore()
    greet = [z_up, z_down, sibling, x_dev[0], x_dev[1]]
    for o in range(1, NY):
        greet.append({"expert": group[o]})
        greet.append({"expert": group[o], "tensor": z * 2 + other})
    for peer in greet:
        pl.semaphore_signal(barrier, inc=1, device_id=peer, device_id_type=MESH)

    loads = [
        pltpu.make_async_copy(tok_hbm, src.at[0], load_sem.at[0]),
        pltpu.make_async_copy(go_hbm, src.at[1], load_sem.at[1]),
        pltpu.make_async_copy(wg_hbm, w.at[0], load_sem.at[2]),
        pltpu.make_async_copy(wu_hbm, w.at[1], load_sem.at[3]),
        pltpu.make_async_copy(wd_hbm, w.at[2], load_sem.at[4]),
    ]
    labels = pltpu.make_async_copy(lab_hbm, lab_ref, load_sem.at[5])
    labels.start()
    for copy in loads:
        copy.start()

    earlier = jnp.where(
        lax.broadcasted_iota(jnp.int32, (TOK, TOK), 0)
        < lax.broadcasted_iota(jnp.int32, (TOK, TOK), 1),
        1.0,
        0.0,
    ).astype(BF)
    labels.wait()
    lab = lab_ref[...]
    onehot = jnp.where(
        lax.broadcasted_iota(jnp.int32, (8, TOK), 0) == lab, 1.0, 0.0
    )
    rank = jnp.sum(nn(onehot.astype(BF), earlier) * onehot, axis=0, keepdims=True)
    relative = ((lab >> 1) - g + NY) & (NY - 1)
    place = relative.astype(F32) * float(SHARE) + rank
    place = place + jnp.where(rank >= float(SHARE), float(HALF - SHARE), 0.0)
    spot = lax.broadcasted_iota(jnp.int32, (ROWS, TOK), 0).astype(F32)
    for j in range(2):
        mine = jnp.where((lab & 1) == j, place, -1.0)
        slots[j] = jnp.where(spot == mine, 1.0, 0.0).astype(BF)

    span = pl.ds(pl.multiple_of(lax.rem(z, 2) * PART, PART), PART)
    y_copies = {}

    def own(first, count):
        return pl.ds(pl.multiple_of(c * HALF + first * SHARE, 16), count * SHARE)

    def quarter(parity, way):
        start = parity * PART + way * (PART // 2)
        return pl.ds(pl.multiple_of(start, PART // 2), PART // 2)

    def pick(k):
        loads[k].wait()
        for j in range(2):
            outgo[k, j] = nn(slots[j, own(1, NY - 1)], src[k, :, span]).astype(BF)

    def remote(source, target, send, recv, device):
        pltpu.make_async_remote_copy(source, target, send, recv, device, MESH).start()

    onward = {"expert": lax.rem(g + 1 + 2 * c, NY)}
    other_span = pl.ds(pl.multiple_of(PART - lax.rem(z, 2) * PART, PART), PART)

    def launch_far(k):
        remote(outgo.at[k, :, pl.ds(SHARE, SHARE)], passing.at[k], s_y, y_r.at[k, 2], onward)

    def launch_near(k):
        for o in (1, 3):
            remote(
                outgo.at[k, :, pl.ds((o - 1) * SHARE, SHARE)],
                x.at[k, :, own(NY - o, 1), span],
                s_y, y_r.at[k, NY - o], {"expert": group[o]},
            )

    def pass_on(k):
        take(passing.at[k], y_r.at[k, 2])
        remote(passing.at[k], x.at[k, :, own(2, 1), span], s_y, y_r.at[k, 0], onward)

    def own_rows(k):
        for j in range(2):
            both = jnp.concatenate([slots[j, pl.ds(0, SHARE)], slots[j, pl.ds(HALF, SHARE)]], axis=0)
            value = nn(both, src[k]).astype(BF)
            x[k, j, pl.ds(0, SHARE)] = value[:SHARE]
            x[k, j, pl.ds(HALF, SHARE)] = value[SHARE:]

    def twin(k, block, columns):
        part_ref = x.at[k, :, own(block, 1), columns]
        remote(part_ref, part_ref, s_w, w_r.at[k], sibling)

    def spread(k, block):
        take(x.at[k, :, own(block, 1), span], y_r.at[k, 0 if block == 2 else block])
        for way in (0, 1):
            part_ref = x.at[k, :, own(block, 1), quarter(lax.rem(z, 2), way)]
            remote(part_ref, part_ref, s_z, z_r.at[k, block - 1], (z_up, z_down)[way])
        twin(k, block, span)

    def collect(k, block):
        take(x.at[k, :, own(block, 1), other_span], z_r.at[k, block - 1])
        twin(k, block, other_span)

    def complete(k):
        theirs_x = pl.ds(pl.multiple_of(other * HALF + SHARE, 16), HALF - SHARE)
        take(x.at[k, :, theirs_x], w_r.at[k])

    def partial(k):
        for j in range(2):
            value = nt(w[k, j], x[1 if k == 2 else 0, j])
            part[k, j] = value
            part16[k, j] = value.astype(BF)
            way = j
            remote(part16.at[k, j, rows(far)], land.at[k, way], s_b, v_r.at[k, way], x_dev[way])
            way = 1 - j
            remote(
                part16.at[k, j, rows((right, left)[way])], land.at[k, 2 + 2 * way + j],
                s_b, b_r.at[k], x_dev[way],
            )

    def join(k):
        for way in (0, 1):
            take(land.at[k, way], v_r.at[k, way])
            near = rows((right, left)[way])
            joined[k, way] = (part[k, way, near] + land[k, way].astype(F32)).astype(BF)
            remote(joined.at[k, way], land.at[k, 2 + 2 * way + way], s_b, b_r.at[k], x_dev[way])

    def arrived(k):
        take(land.at[k, pl.ds(2, 4)], b_r.at[k])

    def total(k, j):
        return part[k, j, rows(d)] + land[k, 2 + j].astype(F32) + land[k, 4 + j].astype(F32)

    def share(n, way, j):
        block = acts.at[n, j, rows(d)]
        recv = c_r.at[n, way] if way == j else f_r.at[n, j]
        remote(block, block, s_c, recv, x_dev[way])

    def relay(n, way):
        block = acts.at[n, way, rows((left, right)[way])]
        take(block, c_r.at[n, way])
        remote(block, block, s_c, f_r.at[n, way], x_dev[way])

    def shared(n, j):
        take(land.at[n, pl.ds(0, 2)], f_r.at[n, j])

    def forward_acts():
        for j in range(2):
            gate = total(0, j)
            up = total(1, j)
            sig = jax.nn.sigmoid(gate)
            active = gate * sig
            acts[0, j, rows(d)] = (active * up).astype(BF)
            share(0, j, j)
            share(0, 1 - j, j)
            keep[0, j] = up * (sig * (1.0 + gate * (1.0 - sig)))
            keep[1, j] = active

    def backward_acts():
        for j in range(2):
            back = total(2, j)
            acts[1, j, rows(d)] = (back * keep[0, j]).astype(BF)
            acts[2, j, rows(d)] = (back * keep[1, j]).astype(BF)
            if j == 0:
                share(1, 0, 0)
                share(2, 0, 0)
            share(1, 1, j)
            share(2, 1, j)

    def late_share():
        share(1, 0, 1)
        share(2, 0, 1)

    def rows_of(kd, j, columns):
        if kd == 0:
            return tn(acts[0, j], w[2, j, :, columns])
        return tn(acts[1, j], w[0, j, :, columns]) + tn(acts[2, j], w[1, j, :, columns])

    mine = pl.ds(pl.multiple_of(c * HALF, 16), HALF)
    theirs = pl.ds(pl.multiple_of(other * HALF, 16), HALF)
    counts = ((4, 3), (3, 4))

    def target(j, way, i):
        ahead = counts[j][way] - i
        return lax.rem(z + (ahead if way == 0 else NZ - ahead), NZ)

    def early(kd, j):
        for way in (0, 1):
            early_out[kd, j, way] = rows_of(kd, j, cols(target(j, way, 0)))
        remote(early_out.at[kd, j, :, theirs], early_in.at[kd, j], s_e, e_r.at[kd, j], sibling)

    def expand(kd, j):
        rows_out[kd, j] = rows_of(kd, j, slice(None))
        remote(rows_out.at[kd, j, theirs], twin_in.at[kd, j], s_t, t_r.at[kd, j], sibling)

    def chunk_sum(kd, j, q):
        return rows_out[kd, j, mine, cols(q)] + twin_in[kd, j, :, cols(q)]

    def ring_number(j, way, i):
        return i + (counts[j][0] if way else 0)

    def reduce_step(kd, j, i):
        if i == 0:
            take(early_in.at[kd, j], e_r.at[kd, j])
        if i == 1:
            take(twin_in.at[kd, j], t_r.at[kd, j])
        for way in (0, 1):
            if i >= counts[j][way]:
                continue
            number = ring_number(j, way, i)
            if i == 0:
                value = early_out[kd, j, way, mine] + early_in[kd, j, way]
            else:
                value = chunk_sum(kd, j, target(j, way, i))
                take(ring_in.at[kd, j, number - 1], r_r.at[kd, j, number - 1])
                value = value + ring_in[kd, j, number - 1].astype(F32)
            ring_out[kd, j, number] = value.astype(BF)
            remote(
                ring_out.at[kd, j, number], ring_in.at[kd, j, number],
                s_r, r_r.at[kd, j, number], (z_up, z_down)[way],
            )

    def go_home(kd, j):
        value = chunk_sum(kd, j, z)
        for way in (0, 1):
            number = ring_number(j, way, counts[j][way] - 1)
            take(ring_in.at[kd, j, number], r_r.at[kd, j, number])
            value = value + ring_in[kd, j, number].astype(F32)
        value = value.astype(BF)
        final[kd, j] = value
        home[kd, j, own(0, 1)] = value[:SHARE]
        for o in (2, 1, 3, 0):
            for same in (0, 1):
                if o == 0 and same == 0:
                    continue
                core = c if same == 0 else other
                remote(
                    final.at[kd, j, pl.ds(o * SHARE, SHARE)],
                    home.at[kd, j, own((NY - o) % NY, 1)],
                    s_h, h_r.at[kd],
                    {"expert": group[o], "tensor": z * 2 + core},
                )

    LANES = 2

    def band(n):
        size = TOK // 2 // LANES
        return pl.ds(pl.multiple_of(c * (TOK // 2) + n * size, size), size)

    outs = [
        [
            RingGather(
                lambda q, kd=kd, n=n: out.at[kd, band(n), cols(q)],
                z,
                z_up,
                z_down,
                sibling,
                (s_gz, gz_r.at[kd, n], s_gs, gs_r.at[kd]),
                *counts[n % 2],
            )
            for n in range(LANES)
        ]
        for kd in range(2)
    ]

    half = pl.ds(pl.multiple_of(c * (TOK // 2), TOK // 2), TOK // 2)
    other_half = pl.ds(pl.multiple_of(other * (TOK // 2), TOK // 2), TOK // 2)

    def settle(kd):
        take(ring_in.at[kd, :, :, pl.ds(0, SHARE)], h_r.at[kd])
        value = tn(slots[0, :, half], home[kd, 0]) + tn(slots[1, :, half], home[kd, 1])
        out[kd, half, cols(z)] = value.astype(BF)
        for lane in outs[kd]:
            lane.start()

    def circulate(kd, hop):
        for lane in outs[kd]:
            lane.step(hop)

    def weight_grad(n, k, j):
        wgrad[n, j] = nn(acts[n, j], x[k, j]).astype(BF)

    def finish(kd):
        take(out.at[kd, other_half], gs_r.at[kd])

    def drain():
        take(x.at[:, :, pl.ds(0, HALF), pl.ds(0, PART)], s_y)
        take(x.at[:, :, pl.ds(0, HALF - SHARE), pl.ds(0, PART)], s_z)
        take(x.at[:, :, pl.ds(0, HALF - SHARE)], s_w)
        take(land, s_b)
        take(land, s_c)
        take(twin_in, s_t)
        take(early_in, s_e)
        take(ring_in, s_r)
        take(ring_in.at[:, :, :, pl.ds(0, SHARE)], s_h)
        take(ring_in.at[:, :, :, pl.ds(0, TOK // 2 // LANES)], s_gz)
        take(out.at[:, half], s_gs)

    pick(0)
    pl.semaphore_wait(barrier, len(greet))
    launch_far(0)
    own_rows(0)
    pick(1)
    launch_near(0)
    pass_on(0)
    launch_far(1)
    spread(0, 3)
    spread(0, 1)
    launch_near(1)
    own_rows(1)
    spread(0, 2)
    pass_on(1)
    collect(0, 3)
    collect(0, 1)
    collect(0, 2)
    spread(1, 3)
    spread(1, 1)
    spread(1, 2)
    complete(0)
    loads[2].wait()
    partial(0)
    collect(1, 3)
    collect(1, 1)
    loads[3].wait()
    partial(1)
    collect(1, 2)
    join(0)
    complete(1)
    loads[4].wait()
    join(1)
    partial(2)
    arrived(0)
    arrived(1)
    forward_acts()
    join(2)
    relay(0, 0)
    relay(0, 1)
    arrived(2)
    backward_acts()
    shared(0, 0)
    shared(0, 1)
    early(0, 0)
    early(0, 1)
    expand(0, 0)
    expand(0, 1)
    reduce_step(0, 0, 0)
    reduce_step(0, 1, 0)
    relay(1, 0)
    weight_grad(0, 1, 0)
    relay(2, 0)
    late_share()
    weight_grad(0, 1, 1)
    reduce_step(0, 0, 1)
    reduce_step(0, 1, 1)
    relay(1, 1)
    relay(2, 1)
    shared(1, 0)
    shared(2, 0)
    early(1, 0)
    expand(1, 0)
    reduce_step(1, 0, 0)
    reduce_step(0, 0, 2)
    reduce_step(0, 1, 2)
    shared(1, 1)
    shared(2, 1)
    early(1, 1)
    expand(1, 1)
    reduce_step(1, 1, 0)
    reduce_step(1, 0, 1)
    reduce_step(0, 0, 3)
    reduce_step(0, 1, 3)
    weight_grad(1, 0, 0)
    reduce_step(1, 1, 1)
    reduce_step(1, 0, 2)
    weight_grad(1, 0, 1)
    go_home(0, 0)
    go_home(0, 1)
    reduce_step(1, 1, 2)
    reduce_step(1, 0, 3)
    weight_grad(2, 0, 0)
    settle(0)
    reduce_step(1, 1, 3)
    go_home(1, 0)
    weight_grad(2, 0, 1)
    circulate(0, 0)
    go_home(1, 1)
    circulate(0, 1)
    settle(1)
    circulate(0, 2)
    circulate(1, 0)
    circulate(0, 3)
    circulate(1, 1)
    circulate(1, 2)
    finish(0)
    circulate(1, 3)
    finish(1)
    drain()


def writer(out, wgrad, mix_hbm, gt_hbm, gg_hbm, gu_hbm, gd_hbm, sems):
    pairs = []
    for j in range(2):
        pairs.append((wgrad.at[1, j], gg_hbm.at[j]))
        pairs.append((wgrad.at[2, j], gu_hbm.at[j]))
        pairs.append((wgrad.at[0, j], gd_hbm.at[j]))
    pairs.append((out.at[0], mix_hbm))
    pairs.append((out.at[1], gt_hbm))
    copies = [pltpu.make_async_copy(a, b, sems.at[i]) for i, (a, b) in enumerate(pairs)]
    for copy in copies:
        copy.start()
    for copy in copies:
        copy.wait()


def body(tokens, labels, grad_out, w_gate, w_up, w_down):
    dma = pltpu.SemaphoreType.DMA
    scratch = [
        pltpu.VMEM((1, TOK), jnp.int32),
        pltpu.VMEM((2, TOK, FEAT), BF),
        pltpu.VMEM((3, 2, HID, FEAT), BF),
        pltpu.VMEM((2, ROWS, TOK), BF),
        pltpu.VMEM((2, 2, HALF - SHARE, PART), BF),
        pltpu.VMEM((2, 2, SHARE, PART), BF),
        pltpu.VMEM((2, 2, ROWS, FEAT), BF),
        pltpu.VMEM((3, 2, HID, ROWS), F32),
        pltpu.VMEM((3, 2, HID, ROWS), BF),
        pltpu.VMEM((3, 6, SLICE, ROWS), BF),
        pltpu.VMEM((3, 2, SLICE, ROWS), BF),
        pltpu.VMEM((3, 2, HID, ROWS), BF),
        pltpu.VMEM((2, 2, SLICE, ROWS), F32),
        pltpu.VMEM((2, 2, HALF, FEAT), F32),
        pltpu.VMEM((2, 2, 2, HALF, COL), F32),
        pltpu.VMEM((2, 2, 2, ROWS, COL), F32),
        pltpu.VMEM((2, 2, ROWS, FEAT), F32),
        pltpu.VMEM((2, 2, 7, HALF, COL), BF),
        pltpu.VMEM((2, 2, 7, HALF, COL), BF),
        pltpu.VMEM((2, 2, HALF, COL), BF),
        pltpu.VMEM((2, 2, ROWS, COL), BF),
        dma((6,)),
        dma((11,)),
        dma((2, 4)),
        dma((2, 3)),
        dma((2,)),
        dma((3, 2)),
        dma((3,)),
        dma((3, 2)),
        dma((3, 2)),
        dma((2, 2)),
        dma((2, 2)),
        dma((2, 2, 7)),
        dma((2,)),
        dma((2, 2, 7)),
        dma((2,)),
    ]
    hbm = pl.BlockSpec(memory_space=pltpu.HBM)
    vmem = pl.BlockSpec(memory_space=pltpu.VMEM)
    out, wgrad = pl.pallas_call(
        kernel,
        out_shape=(
            pltpu.VMEM((2, TOK, FEAT), BF),
            pltpu.VMEM((3, 2, HID, FEAT), BF),
        ),
        in_specs=[hbm] * 6,
        out_specs=(vmem, vmem),
        scratch_shapes=scratch,
        compiler_params=pltpu.CompilerParams(
            collective_id=0, has_side_effects=True, vmem_limit_bytes=50 * 1024 * 1024
        ),
    )(
        labels.reshape(1, TOK),
        tokens,
        grad_out,
        jnp.swapaxes(w_gate, 1, 2),
        jnp.swapaxes(w_up, 1, 2),
        w_down,
    )
    out = pltpu.with_memory_space_constraint(out, pltpu.VMEM)
    wgrad = pltpu.with_memory_space_constraint(wgrad, pltpu.VMEM)
    weights = jax.ShapeDtypeStruct((2, HID, FEAT), BF)
    acts = jax.ShapeDtypeStruct((TOK, FEAT), BF)
    mixed, grad_tokens, gate_t, up_t, down = pl.pallas_call(
        writer,
        out_shape=(acts, acts, weights, weights, weights),
        in_specs=[vmem, vmem],
        out_specs=(hbm,) * 5,
        scratch_shapes=[dma((8,))],
        compiler_params=pltpu.CompilerParams(vmem_limit_bytes=4 * 1024 * 1024),
    )(out, wgrad)
    return mixed, grad_tokens, jnp.swapaxes(gate_t, 1, 2), jnp.swapaxes(up_t, 1, 2), down


def solution(mesh):
    in_specs = (
        P("expert", "dp"),
        P("expert", None),
        P("expert", "dp"),
        P("expert", "dp", "tensor"),
        P("expert", "dp", "tensor"),
        P("expert", "tensor", "dp"),
    )
    out_specs = (
        P("expert", "dp"),
        P("expert", "dp"),
        P("expert", "dp", "tensor"),
        P("expert", "dp", "tensor"),
        P("expert", "tensor", "dp"),
    )
    return jax.shard_map(body, mesh=mesh, in_specs=in_specs, out_specs=out_specs, check_vma=False)
```

```python
import jax
import jax.numpy as jnp
from jax import lax
from jax.experimental import pallas as pl
from jax.experimental.pallas import tpu as pltpu
from jax.sharding import PartitionSpec as P

MOST = 96
NX, NY, NZ = 4, 4, 8
TOK = 512
FEAT = 1024
HID = 448
SLICE = HID // NX
ROWS = NY * MOST
COL = FEAT // NZ
PART = FEAT // 2
SHARE = MOST // 2
HALF = NY * SHARE
BF = jnp.bfloat16
F32 = jnp.float32
MESH = pl.DeviceIdType.MESH


def nt(a, b):
    return lax.dot_general(a, b, (((1,), (1,)), ((), ())), preferred_element_type=F32)


def tn(a, b):
    return lax.dot_general(a, b, (((0,), (0,)), ((), ())), preferred_element_type=F32)


def nn(a, b):
    return jnp.dot(a, b, preferred_element_type=F32)


def take(ref, sem):
    pltpu.make_async_copy(ref, ref, sem).wait()


class RingGather:
    def __init__(self, region, z, right, left, sibling, sems, plus, minus):
        self.region, self.z = region, z
        self.dev = (right, left)
        self.sibling = sibling
        self.zs, self.zr, self.ss, self.sr = sems
        self.count = (plus, minus)

    def chunk(self, way, hop):
        return lax.rem(self.z + (NZ - hop if way == 0 else hop), NZ)

    def number(self, way, hop):
        return hop + (self.count[0] if way else 0)

    def send(self, way, hop):
        part = self.region(self.chunk(way, hop))
        pltpu.make_async_remote_copy(
            part, part, self.zs, self.zr.at[self.number(way, hop)], self.dev[way], MESH
        ).start()

    def twin(self, chunk):
        part = self.region(chunk)
        pltpu.make_async_remote_copy(part, part, self.ss, self.sr, self.sibling, MESH).start()

    def start(self):
        for way in (0, 1):
            self.send(way, 0)
        self.twin(self.z)

    def step(self, hop):
        for way in (0, 1):
            if hop < self.count[way]:
                chunk = self.chunk(way, hop + 1)
                take(self.region(chunk), self.zr.at[self.number(way, hop)])
                if hop + 1 < self.count[way]:
                    self.send(way, hop + 1)
                self.twin(chunk)


def kernel(
    lab_hbm,
    tok_hbm,
    go_hbm,
    wg_hbm,
    wu_hbm,
    wd_hbm,
    out,
    wgrad,
    lab_ref,
    src,
    w,
    slots,
    outgo,
    passing,
    x,
    part,
    part16,
    land,
    joined,
    acts,
    keep,
    twin_in,
    early_in,
    early_out,
    rows_out,
    ring_out,
    ring_in,
    final,
    home,
    load_sem,
    sent,
    y_r,
    z_r,
    w_r,
    v_r,
    b_r,
    c_r,
    f_r,
    t_r,
    e_r,
    r_r,
    h_r,
    gz_r,
    gs_r,
):
    d = lax.axis_index("dp")
    g = lax.axis_index("expert")
    t = lax.axis_index("tensor")
    z = lax.div(t, 2)
    c = lax.rem(t, 2)
    other = 1 - c
    right = lax.rem(d + 1, NX)
    left = lax.rem(d + NX - 1, NX)
    far = lax.rem(d + 2, NX)
    z_up = {"tensor": lax.rem(z + 1, NZ) * 2 + c}
    z_down = {"tensor": lax.rem(z + NZ - 1, NZ) * 2 + c}
    sibling = {"tensor": z * 2 + other}
    x_dev = ({"dp": right}, {"dp": left})
    s_y, s_z, s_w, s_b, s_c, s_t, s_e, s_r, s_h, s_gz, s_gs = [sent.at[i] for i in range(11)]
    group = [lax.rem(g + o, NY) for o in range(NY)]

    def cols(q):
        return pl.ds(pl.multiple_of(q * COL, COL), COL)

    def rows(q):
        return pl.ds(pl.multiple_of(q * SLICE, 16), SLICE)

    barrier = pltpu.get_barrier_semaphore()
    greet = [z_up, z_down, sibling, x_dev[0], x_dev[1]]
    for o in range(1, NY):
        greet.append({"expert": group[o]})
        greet.append({"expert": group[o], "tensor": z * 2 + other})
    for peer in greet:
        pl.semaphore_signal(barrier, inc=1, device_id=peer, device_id_type=MESH)

    loads = [
        pltpu.make_async_copy(tok_hbm, src.at[0], load_sem.at[0]),
        pltpu.make_async_copy(go_hbm, src.at[1], load_sem.at[1]),
        pltpu.make_async_copy(wg_hbm, w.at[0], load_sem.at[2]),
        pltpu.make_async_copy(wu_hbm, w.at[1], load_sem.at[3]),
        pltpu.make_async_copy(wd_hbm, w.at[2], load_sem.at[4]),
    ]
    labels = pltpu.make_async_copy(lab_hbm, lab_ref, load_sem.at[5])
    labels.start()
    for copy in loads:
        copy.start()

    earlier = jnp.where(
        lax.broadcasted_iota(jnp.int32, (TOK, TOK), 0)
        < lax.broadcasted_iota(jnp.int32, (TOK, TOK), 1),
        1.0,
        0.0,
    ).astype(BF)
    labels.wait()
    lab = lab_ref[...]
    onehot = jnp.where(
        lax.broadcasted_iota(jnp.int32, (8, TOK), 0) == lab, 1.0, 0.0
    )
    rank = jnp.sum(nn(onehot.astype(BF), earlier) * onehot, axis=0, keepdims=True)
    relative = ((lab >> 1) - g + NY) & (NY - 1)
    place = relative.astype(F32) * float(SHARE) + rank
    place = place + jnp.where(rank >= float(SHARE), float(HALF - SHARE), 0.0)
    spot = lax.broadcasted_iota(jnp.int32, (ROWS, TOK), 0).astype(F32)
    for j in range(2):
        mine = jnp.where((lab & 1) == j, place, -1.0)
        slots[j] = jnp.where(spot == mine, 1.0, 0.0).astype(BF)

    span = pl.ds(pl.multiple_of(lax.rem(z, 2) * PART, PART), PART)
    y_copies = {}

    def own(first, count):
        return pl.ds(pl.multiple_of(c * HALF + first * SHARE, 16), count * SHARE)

    def quarter(parity, way):
        start = parity * PART + way * (PART // 2)
        return pl.ds(pl.multiple_of(start, PART // 2), PART // 2)

    parcels = ((0, 0, 1), (0, 1, 1), (1, 0, 2))
    present = set()

    def loaded(number):
        if number not in present:
            present.add(number)
            loads[number].wait()

    def pick(p):
        k, first, count = parcels[p]
        loaded(k)
        for j in range(first, first + count):
            outgo[k, j] = nn(slots[j, own(1, NY - 1)], src[k, :, span]).astype(BF)

    def remote(source, target, send, recv, device):
        pltpu.make_async_remote_copy(source, target, send, recv, device, MESH).start()

    onward = {"expert": lax.rem(g + 1 + 2 * c, NY)}
    other_span = pl.ds(pl.multiple_of(PART - lax.rem(z, 2) * PART, PART), PART)

    def outgoing(p, o):
        k, first, count = parcels[p]
        return outgo.at[k, pl.ds(first, count), pl.ds((o - 1) * SHARE, SHARE)]

    def passage(p):
        k, first, count = parcels[p]
        return passing.at[k, pl.ds(first, count)]

    def landed(p, block, columns):
        k, first, count = parcels[p]
        return x.at[k, pl.ds(first, count), own(block, 1), columns]

    def launch_far(p):
        remote(outgoing(p, 2), passage(p), s_y, y_r.at[p, 2], onward)

    def launch_near(p):
        for o in (1, 3):
            remote(
                outgoing(p, o), landed(p, NY - o, span), s_y, y_r.at[p, NY - o], {"expert": group[o]}
            )

    def pass_on(p):
        take(passage(p), y_r.at[p, 2])
        remote(passage(p), landed(p, 2, span), s_y, y_r.at[p, 0], onward)

    def own_rows(k):
        loaded(k)
        for j in range(2):
            both = jnp.concatenate([slots[j, pl.ds(0, SHARE)], slots[j, pl.ds(HALF, SHARE)]], axis=0)
            value = nn(both, src[k]).astype(BF)
            x[k, j, pl.ds(0, SHARE)] = value[:SHARE]
            x[k, j, pl.ds(HALF, SHARE)] = value[SHARE:]

    def twin(p, block, columns):
        remote(landed(p, block, columns), landed(p, block, columns), s_w, w_r.at[p], sibling)

    def spread(p, block):
        take(landed(p, block, span), y_r.at[p, 0 if block == 2 else block])
        for way in (0, 1):
            part_ref = landed(p, block, quarter(lax.rem(z, 2), way))
            remote(part_ref, part_ref, s_z, z_r.at[p, block - 1], (z_up, z_down)[way])
        twin(p, block, span)

    def collect(p, block):
        take(landed(p, block, other_span), z_r.at[p, block - 1])
        twin(p, block, other_span)

    def complete(p):
        k, first, count = parcels[p]
        theirs_x = pl.ds(pl.multiple_of(other * HALF + SHARE, 16), HALF - SHARE)
        take(x.at[k, pl.ds(first, count), theirs_x], w_r.at[p])

    def way_in(k, j):
        return j ^ (k & 1)

    def way_out(n, j):
        return (1 - j, j, 1 - j)[n]

    sides = (right, left)

    def partial(k, j):
        loaded(2 + k)
        value = nt(w[k, j], x[1 if k == 2 else 0, j])
        part[k, j] = value
        part16[k, j] = value.astype(BF)
        way = way_in(k, j)
        remote(part16.at[k, j, rows(far)], land.at[k, j, 0], s_b, v_r.at[k, j], x_dev[way])
        way = 1 - way
        remote(
            part16.at[k, j, rows(sides[way])], land.at[k, j, 1], s_b, b_r.at[k, j], x_dev[way]
        )

    def join(k, j):
        take(land.at[k, j, 0], v_r.at[k, j])
        way = way_in(k, j)
        joined[k, j] = (part[k, j, rows(sides[way])] + land[k, j, 0].astype(F32)).astype(BF)
        remote(joined.at[k, j], land.at[k, j, 2], s_b, b_r.at[k, j], x_dev[way])

    def total(k, j):
        take(land.at[k, j, pl.ds(1, 2)], b_r.at[k, j])
        return part[k, j, rows(d)] + land[k, j, 1].astype(F32) + land[k, j, 2].astype(F32)

    def share(n, j, direct):
        block = acts.at[n, j, rows(d)]
        way = way_out(n, j)
        if direct:
            remote(block, block, s_c, f_r.at[n, j], x_dev[1 - way])
        else:
            remote(block, block, s_c, c_r.at[n, j], x_dev[way])

    def relay(n, j):
        way = way_out(n, j)
        block = acts.at[n, j, rows((left, right)[way])]
        take(block, c_r.at[n, j])
        remote(block, block, s_c, f_r.at[n, j], x_dev[way])

    gathered = set()

    def shared(n, j):
        if (n, j) not in gathered:
            gathered.add((n, j))
            take(land.at[n, 0, pl.ds(0, 2)], f_r.at[n, j])

    def forward_acts(j):
        gate = total(0, j)
        up = total(1, j)
        sig = jax.nn.sigmoid(gate)
        active = gate * sig
        acts[0, j, rows(d)] = (active * up).astype(BF)
        share(0, j, False)
        share(0, j, True)
        keep[0, j] = up * (sig * (1.0 + gate * (1.0 - sig)))
        keep[1, j] = active

    def backward_acts(j):
        back = total(2, j)
        acts[1, j, rows(d)] = (back * keep[0, j]).astype(BF)
        acts[2, j, rows(d)] = (back * keep[1, j]).astype(BF)
        for direct in (False, True):
            share(1, j, direct)
            share(2, j, direct)

    def rows_of(kd, j, columns):
        if kd == 0:
            return tn(acts[0, j], w[2, j, :, columns])
        return tn(acts[1, j], w[0, j, :, columns]) + tn(acts[2, j], w[1, j, :, columns])

    mine = pl.ds(pl.multiple_of(c * HALF, 16), HALF)
    theirs = pl.ds(pl.multiple_of(other * HALF, 16), HALF)
    counts = ((4, 3), (3, 4))

    def target(j, way, i):
        ahead = counts[j][way] - i
        return lax.rem(z + (ahead if way == 0 else NZ - ahead), NZ)

    def ready(kd, j):
        for n in ((0,), (1, 2))[kd]:
            shared(n, j)

    def early(kd, j):
        ready(kd, j)
        for way in (0, 1):
            early_out[kd, j, way] = rows_of(kd, j, cols(target(j, way, 0)))
        remote(early_out.at[kd, j, :, theirs], early_in.at[kd, j], s_e, e_r.at[kd, j], sibling)

    def expand(kd, j):
        ready(kd, j)
        rows_out[kd, j] = rows_of(kd, j, slice(None))
        remote(rows_out.at[kd, j, theirs], twin_in.at[kd, j], s_t, t_r.at[kd, j], sibling)

    def chunk_sum(kd, j, q):
        return rows_out[kd, j, mine, cols(q)] + twin_in[kd, j, :, cols(q)]

    def ring_number(j, way, i):
        return i + (counts[j][0] if way else 0)

    def reduce_step(kd, j, i):
        if i == 0:
            take(early_in.at[kd, j], e_r.at[kd, j])
        if i == 1:
            take(twin_in.at[kd, j], t_r.at[kd, j])
        for way in (0, 1):
            if i >= counts[j][way]:
                continue
            number = ring_number(j, way, i)
            if i == 0:
                value = early_out[kd, j, way, mine] + early_in[kd, j, way]
            else:
                value = chunk_sum(kd, j, target(j, way, i))
                take(ring_in.at[kd, j, number - 1], r_r.at[kd, j, number - 1])
                value = value + ring_in[kd, j, number - 1].astype(F32)
            ring_out[kd, j, number] = value.astype(BF)
            remote(
                ring_out.at[kd, j, number], ring_in.at[kd, j, number],
                s_r, r_r.at[kd, j, number], (z_up, z_down)[way],
            )

    def go_home(kd, j):
        value = chunk_sum(kd, j, z)
        for way in (0, 1):
            number = ring_number(j, way, counts[j][way] - 1)
            take(ring_in.at[kd, j, number], r_r.at[kd, j, number])
            value = value + ring_in[kd, j, number].astype(F32)
        value = value.astype(BF)
        final[kd, j] = value
        home[kd, j, own(0, 1)] = value[:SHARE]
        for o in (2, 1, 3, 0):
            for same in (0, 1):
                if o == 0 and same == 0:
                    continue
                core = c if same == 0 else other
                remote(
                    final.at[kd, j, pl.ds(o * SHARE, SHARE)],
                    home.at[kd, j, own((NY - o) % NY, 1)],
                    s_h, h_r.at[kd],
                    {"expert": group[o], "tensor": z * 2 + core},
                )

    LANES = 2

    def band(n):
        size = TOK // 2 // LANES
        return pl.ds(pl.multiple_of(c * (TOK // 2) + n * size, size), size)

    outs = [
        [
            RingGather(
                lambda q, kd=kd, n=n: out.at[kd, band(n), cols(q)],
                z,
                z_up,
                z_down,
                sibling,
                (s_gz, gz_r.at[kd, n], s_gs, gs_r.at[kd]),
                *counts[n % 2],
            )
            for n in range(LANES)
        ]
        for kd in range(2)
    ]

    half = pl.ds(pl.multiple_of(c * (TOK // 2), TOK // 2), TOK // 2)
    other_half = pl.ds(pl.multiple_of(other * (TOK // 2), TOK // 2), TOK // 2)

    def settle(kd):
        take(ring_in.at[kd, :, :, pl.ds(0, SHARE)], h_r.at[kd])
        value = tn(slots[0, :, half], home[kd, 0]) + tn(slots[1, :, half], home[kd, 1])
        out[kd, half, cols(z)] = value.astype(BF)
        for lane in outs[kd]:
            lane.start()

    def circulate(kd, hop):
        for lane in outs[kd]:
            lane.step(hop)

    def weight_grad(n, k, j):
        shared(n, j)
        wgrad[n, j] = nn(acts[n, j], x[k, j]).astype(BF)

    def finish(kd):
        take(out.at[kd, other_half], gs_r.at[kd])

    def drain():
        take(x.at[:, :, pl.ds(0, HALF), pl.ds(0, PART)], s_y)
        take(x.at[:, :, pl.ds(0, HALF - SHARE), pl.ds(0, PART)], s_z)
        take(x.at[:, :, pl.ds(0, HALF - SHARE)], s_w)
        take(land, s_b)
        take(land, s_c)
        take(twin_in, s_t)
        take(early_in, s_e)
        take(ring_in, s_r)
        take(ring_in.at[:, :, :, pl.ds(0, SHARE)], s_h)
        take(ring_in.at[:, :, :, pl.ds(0, TOK // 2 // LANES)], s_gz)
        take(out.at[:, half], s_gs)

    pick(1)
    pl.semaphore_wait(barrier, len(greet))
    launch_far(1)
    launch_near(1)
    pick(0)
    launch_far(0)
    pass_on(1)
    launch_near(0)
    spread(1, 1)
    spread(1, 3)
    pass_on(0)
    pick(2)
    launch_far(2)
    launch_near(2)
    spread(1, 2)
    collect(1, 1)
    spread(0, 3)
    collect(1, 3)
    own_rows(0)
    spread(0, 1)
    collect(1, 2)
    spread(0, 2)
    complete(1)
    partial(0, 1)
    pass_on(2)
    collect(0, 3)
    collect(0, 1)
    partial(1, 1)
    collect(0, 2)
    spread(2, 3)
    complete(0)
    spread(2, 1)
    partial(0, 0)
    partial(1, 0)
    own_rows(1)
    spread(2, 2)
    join(1, 1)
    collect(2, 1)
    join(0, 1)
    join(0, 0)
    collect(2, 3)
    collect(2, 2)
    join(1, 0)
    complete(2)
    partial(2, 1)
    forward_acts(1)
    forward_acts(0)
    join(2, 1)
    partial(2, 0)
    relay(0, 1)
    relay(0, 0)
    join(2, 0)
    backward_acts(1)
    backward_acts(0)
    early(0, 0)
    early(0, 1)
    relay(1, 1)
    relay(2, 1)
    reduce_step(0, 0, 0)
    reduce_step(0, 1, 0)
    expand(0, 1)
    expand(0, 0)
    relay(1, 0)
    reduce_step(0, 0, 1)
    reduce_step(0, 1, 1)
    relay(2, 0)
    weight_grad(0, 1, 0)
    early(1, 1)
    reduce_step(0, 0, 2)
    early(1, 0)
    reduce_step(1, 1, 0)
    expand(1, 1)
    reduce_step(1, 0, 0)
    expand(1, 0)
    reduce_step(0, 1, 2)
    reduce_step(1, 1, 1)
    reduce_step(1, 0, 1)
    reduce_step(0, 1, 3)
    reduce_step(0, 0, 3)
    reduce_step(1, 1, 2)
    weight_grad(2, 0, 0)
    reduce_step(1, 0, 2)
    go_home(0, 1)
    weight_grad(1, 0, 1)
    go_home(0, 0)
    reduce_step(1, 1, 3)
    reduce_step(1, 0, 3)
    settle(0)
    go_home(1, 1)
    go_home(1, 0)
    weight_grad(0, 1, 1)
    circulate(0, 0)
    settle(1)
    circulate(0, 1)
    circulate(1, 0)
    circulate(0, 2)
    circulate(1, 1)
    circulate(0, 3)
    circulate(1, 2)
    weight_grad(1, 0, 0)
    finish(0)
    weight_grad(2, 0, 1)
    circulate(1, 3)
    finish(1)
    drain()


def writer(out, wgrad, mix_hbm, gt_hbm, gg_hbm, gu_hbm, gd_hbm, sems):
    pairs = []
    for j in range(2):
        pairs.append((wgrad.at[1, j], gg_hbm.at[j]))
        pairs.append((wgrad.at[2, j], gu_hbm.at[j]))
        pairs.append((wgrad.at[0, j], gd_hbm.at[j]))
    pairs.append((out.at[0], mix_hbm))
    pairs.append((out.at[1], gt_hbm))
    copies = [pltpu.make_async_copy(a, b, sems.at[i]) for i, (a, b) in enumerate(pairs)]
    for copy in copies:
        copy.start()
    for copy in copies:
        copy.wait()


def body(tokens, labels, grad_out, w_gate, w_up, w_down):
    dma = pltpu.SemaphoreType.DMA
    scratch = [
        pltpu.VMEM((1, TOK), jnp.int32),
        pltpu.VMEM((2, TOK, FEAT), BF),
        pltpu.VMEM((3, 2, HID, FEAT), BF),
        pltpu.VMEM((2, ROWS, TOK), BF),
        pltpu.VMEM((2, 2, HALF - SHARE, PART), BF),
        pltpu.VMEM((2, 2, SHARE, PART), BF),
        pltpu.VMEM((2, 2, ROWS, FEAT), BF),
        pltpu.VMEM((3, 2, HID, ROWS), F32),
        pltpu.VMEM((3, 2, HID, ROWS), BF),
        pltpu.VMEM((3, 2, 3, SLICE, ROWS), BF),
        pltpu.VMEM((3, 2, SLICE, ROWS), BF),
        pltpu.VMEM((3, 2, HID, ROWS), BF),
        pltpu.VMEM((2, 2, SLICE, ROWS), F32),
        pltpu.VMEM((2, 2, HALF, FEAT), F32),
        pltpu.VMEM((2, 2, 2, HALF, COL), F32),
        pltpu.VMEM((2, 2, 2, ROWS, COL), F32),
        pltpu.VMEM((2, 2, ROWS, FEAT), F32),
        pltpu.VMEM((2, 2, 7, HALF, COL), BF),
        pltpu.VMEM((2, 2, 7, HALF, COL), BF),
        pltpu.VMEM((2, 2, HALF, COL), BF),
        pltpu.VMEM((2, 2, ROWS, COL), BF),
        dma((6,)),
        dma((11,)),
        dma((3, 4)),
        dma((3, 3)),
        dma((3,)),
        dma((3, 2)),
        dma((3, 2)),
        dma((3, 2)),
        dma((3, 2)),
        dma((2, 2)),
        dma((2, 2)),
        dma((2, 2, 7)),
        dma((2,)),
        dma((2, 2, 7)),
        dma((2,)),
    ]
    hbm = pl.BlockSpec(memory_space=pltpu.HBM)
    vmem = pl.BlockSpec(memory_space=pltpu.VMEM)
    out, wgrad = pl.pallas_call(
        kernel,
        out_shape=(
            pltpu.VMEM((2, TOK, FEAT), BF),
            pltpu.VMEM((3, 2, HID, FEAT), BF),
        ),
        in_specs=[hbm] * 6,
        out_specs=(vmem, vmem),
        scratch_shapes=scratch,
        compiler_params=pltpu.CompilerParams(
            collective_id=0, has_side_effects=True, vmem_limit_bytes=50 * 1024 * 1024
        ),
    )(
        labels.reshape(1, TOK),
        tokens,
        grad_out,
        jnp.swapaxes(w_gate, 1, 2),
        jnp.swapaxes(w_up, 1, 2),
        w_down,
    )
    out = pltpu.with_memory_space_constraint(out, pltpu.VMEM)
    wgrad = pltpu.with_memory_space_constraint(wgrad, pltpu.VMEM)
    weights = jax.ShapeDtypeStruct((2, HID, FEAT), BF)
    acts = jax.ShapeDtypeStruct((TOK, FEAT), BF)
    mixed, grad_tokens, gate_t, up_t, down = pl.pallas_call(
        writer,
        out_shape=(acts, acts, weights, weights, weights),
        in_specs=[vmem, vmem],
        out_specs=(hbm,) * 5,
        scratch_shapes=[dma((8,))],
        compiler_params=pltpu.CompilerParams(vmem_limit_bytes=4 * 1024 * 1024),
    )(out, wgrad)
    return mixed, grad_tokens, jnp.swapaxes(gate_t, 1, 2), jnp.swapaxes(up_t, 1, 2), down


def solution(mesh):
    in_specs = (
        P("expert", "dp"),
        P("expert", None),
        P("expert", "dp"),
        P("expert", "dp", "tensor"),
        P("expert", "dp", "tensor"),
        P("expert", "tensor", "dp"),
    )
    out_specs = (
        P("expert", "dp"),
        P("expert", "dp"),
        P("expert", "dp", "tensor"),
        P("expert", "dp", "tensor"),
        P("expert", "tensor", "dp"),
    )
    return jax.shard_map(body, mesh=mesh, in_specs=in_specs, out_specs=out_specs, check_vma=False)
```

```python
import jax
import jax.numpy as jnp
from jax import lax
from jax.experimental import pallas as pl
from jax.experimental.pallas import tpu as pltpu
from jax.sharding import PartitionSpec as P

MOST = 96
NX, NY, NZ = 4, 4, 8
TOK = 512
FEAT = 1024
HID = 448
SLICE = HID // NX
ROWS = NY * MOST
COL = FEAT // NZ
PART = FEAT // 2
SHARE = MOST // 2
HALF = NY * SHARE
BF = jnp.bfloat16
F32 = jnp.float32
MESH = pl.DeviceIdType.MESH


def nt(a, b):
    return lax.dot_general(a, b, (((1,), (1,)), ((), ())), preferred_element_type=F32)


def tn(a, b):
    return lax.dot_general(a, b, (((0,), (0,)), ((), ())), preferred_element_type=F32)


def nn(a, b):
    return jnp.dot(a, b, preferred_element_type=F32)


def take(ref, sem):
    pltpu.make_async_copy(ref, ref, sem).wait()


class RingGather:
    def __init__(self, region, z, right, left, sibling, sems, plus, minus):
        self.region, self.z = region, z
        self.dev = (right, left)
        self.sibling = sibling
        self.zs, self.zr, self.ss, self.sr = sems
        self.count = (plus, minus)

    def chunk(self, way, hop):
        return lax.rem(self.z + (NZ - hop if way == 0 else hop), NZ)

    def number(self, way, hop):
        return hop + (self.count[0] if way else 0)

    def send(self, way, hop):
        part = self.region(self.chunk(way, hop))
        pltpu.make_async_remote_copy(
            part, part, self.zs, self.zr.at[self.number(way, hop)], self.dev[way], MESH
        ).start()

    def twin(self, chunk):
        part = self.region(chunk)
        pltpu.make_async_remote_copy(part, part, self.ss, self.sr, self.sibling, MESH).start()

    def start(self):
        for way in (0, 1):
            self.send(way, 0)
        self.twin(self.z)

    def step(self, hop):
        for way in (0, 1):
            if hop < self.count[way]:
                chunk = self.chunk(way, hop + 1)
                take(self.region(chunk), self.zr.at[self.number(way, hop)])
                if hop + 1 < self.count[way]:
                    self.send(way, hop + 1)
                self.twin(chunk)


def kernel(
    lab_hbm,
    tok_hbm,
    go_hbm,
    wg_hbm,
    wu_hbm,
    wd_hbm,
    out,
    wgrad,
    lab_ref,
    src,
    w,
    slots,
    outgo,
    passing,
    x,
    part,
    part16,
    ahead,
    land,
    joined,
    acts,
    keep,
    twin_in,
    early_in,
    early_out,
    rows_out,
    ring_out,
    ring_in,
    final,
    home,
    load_sem,
    sent,
    y_r,
    z_r,
    w_r,
    v_r,
    b_r,
    c_r,
    f_r,
    t_r,
    e_r,
    r_r,
    h_r,
    gz_r,
    gs_r,
):
    d = lax.axis_index("dp")
    g = lax.axis_index("expert")
    t = lax.axis_index("tensor")
    z = lax.div(t, 2)
    c = lax.rem(t, 2)
    other = 1 - c
    right = lax.rem(d + 1, NX)
    left = lax.rem(d + NX - 1, NX)
    far = lax.rem(d + 2, NX)
    z_up = {"tensor": lax.rem(z + 1, NZ) * 2 + c}
    z_down = {"tensor": lax.rem(z + NZ - 1, NZ) * 2 + c}
    sibling = {"tensor": z * 2 + other}
    x_dev = ({"dp": right}, {"dp": left})
    s_y, s_z, s_w, s_b, s_c, s_t, s_e, s_r, s_h, s_gz, s_gs = [sent.at[i] for i in range(11)]
    group = [lax.rem(g + o, NY) for o in range(NY)]

    def cols(q):
        return pl.ds(pl.multiple_of(q * COL, COL), COL)

    def rows(q):
        return pl.ds(pl.multiple_of(q * SLICE, 16), SLICE)

    barrier = pltpu.get_barrier_semaphore()
    greet = [z_up, z_down, sibling, x_dev[0], x_dev[1]]
    for o in range(1, NY):
        greet.append({"expert": group[o]})
        greet.append({"expert": group[o], "tensor": z * 2 + other})
    for peer in greet:
        pl.semaphore_signal(barrier, inc=1, device_id=peer, device_id_type=MESH)

    loads = [
        pltpu.make_async_copy(tok_hbm, src.at[0], load_sem.at[0]),
        pltpu.make_async_copy(go_hbm, src.at[1], load_sem.at[1]),
        pltpu.make_async_copy(wg_hbm, w.at[0], load_sem.at[2]),
        pltpu.make_async_copy(wu_hbm, w.at[1], load_sem.at[3]),
        pltpu.make_async_copy(wd_hbm, w.at[2], load_sem.at[4]),
    ]
    labels = pltpu.make_async_copy(lab_hbm, lab_ref, load_sem.at[5])
    labels.start()
    for copy in loads:
        copy.start()

    earlier = jnp.where(
        lax.broadcasted_iota(jnp.int32, (TOK, TOK), 0)
        < lax.broadcasted_iota(jnp.int32, (TOK, TOK), 1),
        1.0,
        0.0,
    ).astype(BF)
    labels.wait()
    lab = lab_ref[...]
    onehot = jnp.where(
        lax.broadcasted_iota(jnp.int32, (8, TOK), 0) == lab, 1.0, 0.0
    )
    rank = jnp.sum(nn(onehot.astype(BF), earlier) * onehot, axis=0, keepdims=True)
    relative = ((lab >> 1) - g + NY) & (NY - 1)
    place = relative.astype(F32) * float(SHARE) + rank
    place = place + jnp.where(rank >= float(SHARE), float(HALF - SHARE), 0.0)
    spot = lax.broadcasted_iota(jnp.int32, (ROWS, TOK), 0).astype(F32)
    for j in range(2):
        mine = jnp.where((lab & 1) == j, place, -1.0)
        slots[j] = jnp.where(spot == mine, 1.0, 0.0).astype(BF)

    span = pl.ds(pl.multiple_of(lax.rem(z, 2) * PART, PART), PART)
    y_copies = {}

    def own(first, count):
        return pl.ds(pl.multiple_of(c * HALF + first * SHARE, 16), count * SHARE)

    def quarter(parity, way):
        start = parity * PART + way * (PART // 2)
        return pl.ds(pl.multiple_of(start, PART // 2), PART // 2)

    parcels = ((0, 0, 1), (0, 1, 1), (1, 0, 2))
    present = set()

    def loaded(number):
        if number not in present:
            present.add(number)
            loads[number].wait()

    def pick(p):
        k, first, count = parcels[p]
        loaded(k)
        for j in range(first, first + count):
            outgo[k, j] = nn(slots[j, own(1, NY - 1)], src[k, :, span]).astype(BF)

    def remote(source, target, send, recv, device):
        pltpu.make_async_remote_copy(source, target, send, recv, device, MESH).start()

    onward = {"expert": lax.rem(g + 1 + 2 * c, NY)}
    other_span = pl.ds(pl.multiple_of(PART - lax.rem(z, 2) * PART, PART), PART)

    def outgoing(p, o):
        k, first, count = parcels[p]
        return outgo.at[k, pl.ds(first, count), pl.ds((o - 1) * SHARE, SHARE)]

    def passage(p):
        k, first, count = parcels[p]
        return passing.at[k, pl.ds(first, count)]

    def landed(p, block, columns):
        k, first, count = parcels[p]
        return x.at[k, pl.ds(first, count), own(block, 1), columns]

    def launch_far(p):
        remote(outgoing(p, 2), passage(p), s_y, y_r.at[p, 2], onward)

    def launch_near(p):
        for o in (1, 3):
            remote(
                outgoing(p, o), landed(p, NY - o, span), s_y, y_r.at[p, NY - o], {"expert": group[o]}
            )

    def pass_on(p):
        take(passage(p), y_r.at[p, 2])
        remote(passage(p), landed(p, 2, span), s_y, y_r.at[p, 0], onward)

    def own_rows(k):
        loaded(k)
        for j in range(2):
            both = jnp.concatenate([slots[j, pl.ds(0, SHARE)], slots[j, pl.ds(HALF, SHARE)]], axis=0)
            value = nn(both, src[k]).astype(BF)
            x[k, j, pl.ds(0, SHARE)] = value[:SHARE]
            x[k, j, pl.ds(HALF, SHARE)] = value[SHARE:]

    def twin(p, block, columns):
        remote(landed(p, block, columns), landed(p, block, columns), s_w, w_r.at[p], sibling)

    def spread(p, block):
        take(landed(p, block, span), y_r.at[p, 0 if block == 2 else block])
        for way in (0, 1):
            part_ref = landed(p, block, quarter(lax.rem(z, 2), way))
            remote(part_ref, part_ref, s_z, z_r.at[p, block - 1], (z_up, z_down)[way])
        twin(p, block, span)

    def collect(p, block):
        take(landed(p, block, other_span), z_r.at[p, block - 1])
        twin(p, block, other_span)

    def complete(p):
        k, first, count = parcels[p]
        theirs_x = pl.ds(pl.multiple_of(other * HALF + SHARE, 16), HALF - SHARE)
        take(x.at[k, pl.ds(first, count), theirs_x], w_r.at[p])

    def way_in(k, j):
        return j ^ (k & 1)

    def way_out(n, j):
        return (1 - j, j, 1 - j)[n]

    sides = (right, left)
    begun = []

    def partial(k, j):
        loaded(2 + k)
        way = way_in(k, j)
        first = not begun
        if first:
            begun.append((k, j))
            ahead[...] = nt(w[k, j, rows(far)], x[0, j]).astype(BF)
            remote(ahead, land.at[k, j, 0], s_b, v_r.at[k, j], x_dev[way])
        value = nt(w[k, j], x[1 if k == 2 else 0, j])
        part[k, j] = value
        part16[k, j] = value.astype(BF)
        if not first:
            remote(part16.at[k, j, rows(far)], land.at[k, j, 0], s_b, v_r.at[k, j], x_dev[way])
        way = 1 - way
        remote(
            part16.at[k, j, rows(sides[way])], land.at[k, j, 1], s_b, b_r.at[k, j], x_dev[way]
        )

    def join(k, j):
        take(land.at[k, j, 0], v_r.at[k, j])
        way = way_in(k, j)
        joined[k, j] = (part[k, j, rows(sides[way])] + land[k, j, 0].astype(F32)).astype(BF)
        remote(joined.at[k, j], land.at[k, j, 2], s_b, b_r.at[k, j], x_dev[way])

    def total(k, j):
        take(land.at[k, j, pl.ds(1, 2)], b_r.at[k, j])
        return part[k, j, rows(d)] + land[k, j, 1].astype(F32) + land[k, j, 2].astype(F32)

    def share(n, j, direct):
        block = acts.at[n, j, rows(d)]
        way = way_out(n, j)
        if direct:
            remote(block, block, s_c, f_r.at[n, j], x_dev[1 - way])
        else:
            remote(block, block, s_c, c_r.at[n, j], x_dev[way])

    def relay(n, j):
        way = way_out(n, j)
        block = acts.at[n, j, rows((left, right)[way])]
        take(block, c_r.at[n, j])
        remote(block, block, s_c, f_r.at[n, j], x_dev[way])

    gathered = set()

    def shared(n, j):
        if (n, j) not in gathered:
            gathered.add((n, j))
            take(land.at[n, 0, pl.ds(0, 2)], f_r.at[n, j])

    def forward_acts(j):
        gate = total(0, j)
        up = total(1, j)
        sig = jax.nn.sigmoid(gate)
        active = gate * sig
        acts[0, j, rows(d)] = (active * up).astype(BF)
        share(0, j, False)
        share(0, j, True)
        keep[0, j] = up * (sig * (1.0 + gate * (1.0 - sig)))
        keep[1, j] = active

    def backward_acts(j):
        back = total(2, j)
        acts[1, j, rows(d)] = (back * keep[0, j]).astype(BF)
        acts[2, j, rows(d)] = (back * keep[1, j]).astype(BF)
        for direct in (False, True):
            share(1, j, direct)
            share(2, j, direct)

    def rows_of(kd, j, columns):
        if kd == 0:
            return tn(acts[0, j], w[2, j, :, columns])
        return tn(acts[1, j], w[0, j, :, columns]) + tn(acts[2, j], w[1, j, :, columns])

    mine = pl.ds(pl.multiple_of(c * HALF, 16), HALF)
    theirs = pl.ds(pl.multiple_of(other * HALF, 16), HALF)
    counts = ((4, 3), (3, 4))

    def target(j, way, i):
        ahead = counts[j][way] - i
        return lax.rem(z + (ahead if way == 0 else NZ - ahead), NZ)

    def ready(kd, j):
        for n in ((0,), (1, 2))[kd]:
            shared(n, j)

    def early(kd, j):
        ready(kd, j)
        for way in (0, 1):
            early_out[kd, j, way] = rows_of(kd, j, cols(target(j, way, 0)))
        remote(early_out.at[kd, j, :, theirs], early_in.at[kd, j], s_e, e_r.at[kd, j], sibling)

    def expand(kd, j):
        ready(kd, j)
        rows_out[kd, j] = rows_of(kd, j, slice(None))
        remote(rows_out.at[kd, j, theirs], twin_in.at[kd, j], s_t, t_r.at[kd, j], sibling)

    def chunk_sum(kd, j, q):
        return rows_out[kd, j, mine, cols(q)] + twin_in[kd, j, :, cols(q)]

    def ring_number(j, way, i):
        return i + (counts[j][0] if way else 0)

    def reduce_step(kd, j, i):
        if i == 0:
            take(early_in.at[kd, j], e_r.at[kd, j])
        if i == 1:
            take(twin_in.at[kd, j], t_r.at[kd, j])
        for way in (0, 1):
            if i >= counts[j][way]:
                continue
            number = ring_number(j, way, i)
            if i == 0:
                value = early_out[kd, j, way, mine] + early_in[kd, j, way]
            else:
                value = chunk_sum(kd, j, target(j, way, i))
                take(ring_in.at[kd, j, number - 1], r_r.at[kd, j, number - 1])
                value = value + ring_in[kd, j, number - 1].astype(F32)
            ring_out[kd, j, number] = value.astype(BF)
            remote(
                ring_out.at[kd, j, number], ring_in.at[kd, j, number],
                s_r, r_r.at[kd, j, number], (z_up, z_down)[way],
            )

    def go_home(kd, j):
        value = chunk_sum(kd, j, z)
        for way in (0, 1):
            number = ring_number(j, way, counts[j][way] - 1)
            take(ring_in.at[kd, j, number], r_r.at[kd, j, number])
            value = value + ring_in[kd, j, number].astype(F32)
        value = value.astype(BF)
        final[kd, j] = value
        home[kd, j, own(0, 1)] = value[:SHARE]
        for o in (2, 1, 3, 0):
            for same in (0, 1):
                if o == 0 and same == 0:
                    continue
                core = c if same == 0 else other
                remote(
                    final.at[kd, j, pl.ds(o * SHARE, SHARE)],
                    home.at[kd, j, own((NY - o) % NY, 1)],
                    s_h, h_r.at[kd],
                    {"expert": group[o], "tensor": z * 2 + core},
                )

    LANES = 2

    def band(n):
        size = TOK // 2 // LANES
        return pl.ds(pl.multiple_of(c * (TOK // 2) + n * size, size), size)

    outs = [
        [
            RingGather(
                lambda q, kd=kd, n=n: out.at[kd, band(n), cols(q)],
                z,
                z_up,
                z_down,
                sibling,
                (s_gz, gz_r.at[kd, n], s_gs, gs_r.at[kd]),
                *counts[n % 2],
            )
            for n in range(LANES)
        ]
        for kd in range(2)
    ]

    half = pl.ds(pl.multiple_of(c * (TOK // 2), TOK // 2), TOK // 2)
    other_half = pl.ds(pl.multiple_of(other * (TOK // 2), TOK // 2), TOK // 2)

    def settle(kd):
        take(ring_in.at[kd, :, :, pl.ds(0, SHARE)], h_r.at[kd])
        value = tn(slots[0, :, half], home[kd, 0]) + tn(slots[1, :, half], home[kd, 1])
        out[kd, half, cols(z)] = value.astype(BF)
        for lane in outs[kd]:
            lane.start()

    def circulate(kd, hop):
        for lane in outs[kd]:
            lane.step(hop)

    def weight_grad(n, k, j):
        shared(n, j)
        wgrad[n, j] = nn(acts[n, j], x[k, j]).astype(BF)

    def finish(kd):
        take(out.at[kd, other_half], gs_r.at[kd])

    def drain():
        take(x.at[:, :, pl.ds(0, HALF), pl.ds(0, PART)], s_y)
        take(x.at[:, :, pl.ds(0, HALF - SHARE), pl.ds(0, PART)], s_z)
        take(x.at[:, :, pl.ds(0, HALF - SHARE)], s_w)
        take(land, s_b)
        take(land, s_c)
        take(twin_in, s_t)
        take(early_in, s_e)
        take(ring_in, s_r)
        take(ring_in.at[:, :, :, pl.ds(0, SHARE)], s_h)
        take(ring_in.at[:, :, :, pl.ds(0, TOK // 2 // LANES)], s_gz)
        take(out.at[:, half], s_gs)

    pick(1)
    pl.semaphore_wait(barrier, len(greet))
    launch_far(1)
    launch_near(1)
    pick(0)
    launch_far(0)
    pass_on(1)
    launch_near(0)
    spread(1, 1)
    spread(1, 3)
    pass_on(0)
    pick(2)
    launch_far(2)
    launch_near(2)
    spread(1, 2)
    collect(1, 1)
    spread(0, 3)
    collect(1, 3)
    own_rows(0)
    spread(0, 1)
    collect(1, 2)
    spread(0, 2)
    complete(1)
    partial(0, 1)
    pass_on(2)
    collect(0, 3)
    collect(0, 1)
    partial(1, 1)
    collect(0, 2)
    spread(2, 3)
    complete(0)
    spread(2, 1)
    partial(0, 0)
    partial(1, 0)
    own_rows(1)
    spread(2, 2)
    join(1, 1)
    collect(2, 1)
    join(0, 1)
    join(0, 0)
    collect(2, 3)
    collect(2, 2)
    join(1, 0)
    complete(2)
    partial(2, 1)
    forward_acts(1)
    forward_acts(0)
    join(2, 1)
    partial(2, 0)
    relay(0, 1)
    relay(0, 0)
    join(2, 0)
    backward_acts(1)
    backward_acts(0)
    early(0, 0)
    early(0, 1)
    relay(1, 1)
    relay(2, 1)
    reduce_step(0, 0, 0)
    reduce_step(0, 1, 0)
    expand(0, 1)
    expand(0, 0)
    relay(1, 0)
    reduce_step(0, 0, 1)
    reduce_step(0, 1, 1)
    relay(2, 0)
    weight_grad(0, 1, 0)
    early(1, 1)
    reduce_step(0, 0, 2)
    early(1, 0)
    reduce_step(1, 1, 0)
    expand(1, 1)
    reduce_step(1, 0, 0)
    expand(1, 0)
    reduce_step(0, 1, 2)
    reduce_step(1, 1, 1)
    reduce_step(1, 0, 1)
    reduce_step(0, 1, 3)
    reduce_step(0, 0, 3)
    reduce_step(1, 1, 2)
    weight_grad(2, 0, 0)
    reduce_step(1, 0, 2)
    go_home(0, 1)
    weight_grad(1, 0, 1)
    go_home(0, 0)
    reduce_step(1, 1, 3)
    reduce_step(1, 0, 3)
    settle(0)
    go_home(1, 1)
    go_home(1, 0)
    weight_grad(0, 1, 1)
    circulate(0, 0)
    settle(1)
    circulate(0, 1)
    circulate(1, 0)
    circulate(0, 2)
    circulate(1, 1)
    circulate(0, 3)
    circulate(1, 2)
    weight_grad(1, 0, 0)
    finish(0)
    weight_grad(2, 0, 1)
    circulate(1, 3)
    finish(1)
    drain()


def writer(out, wgrad, mix_hbm, gt_hbm, gg_hbm, gu_hbm, gd_hbm, sems):
    pairs = []
    for j in range(2):
        pairs.append((wgrad.at[1, j], gg_hbm.at[j]))
        pairs.append((wgrad.at[2, j], gu_hbm.at[j]))
        pairs.append((wgrad.at[0, j], gd_hbm.at[j]))
    pairs.append((out.at[0], mix_hbm))
    pairs.append((out.at[1], gt_hbm))
    copies = [pltpu.make_async_copy(a, b, sems.at[i]) for i, (a, b) in enumerate(pairs)]
    for copy in copies:
        copy.start()
    for copy in copies:
        copy.wait()


def body(tokens, labels, grad_out, w_gate, w_up, w_down):
    dma = pltpu.SemaphoreType.DMA
    scratch = [
        pltpu.VMEM((1, TOK), jnp.int32),
        pltpu.VMEM((2, TOK, FEAT), BF),
        pltpu.VMEM((3, 2, HID, FEAT), BF),
        pltpu.VMEM((2, ROWS, TOK), BF),
        pltpu.VMEM((2, 2, HALF - SHARE, PART), BF),
        pltpu.VMEM((2, 2, SHARE, PART), BF),
        pltpu.VMEM((2, 2, ROWS, FEAT), BF),
        pltpu.VMEM((3, 2, HID, ROWS), F32),
        pltpu.VMEM((3, 2, HID, ROWS), BF),
        pltpu.VMEM((SLICE, ROWS), BF),
        pltpu.VMEM((3, 2, 3, SLICE, ROWS), BF),
        pltpu.VMEM((3, 2, SLICE, ROWS), BF),
        pltpu.VMEM((3, 2, HID, ROWS), BF),
        pltpu.VMEM((2, 2, SLICE, ROWS), F32),
        pltpu.VMEM((2, 2, HALF, FEAT), F32),
        pltpu.VMEM((2, 2, 2, HALF, COL), F32),
        pltpu.VMEM((2, 2, 2, ROWS, COL), F32),
        pltpu.VMEM((2, 2, ROWS, FEAT), F32),
        pltpu.VMEM((2, 2, 7, HALF, COL), BF),
        pltpu.VMEM((2, 2, 7, HALF, COL), BF),
        pltpu.VMEM((2, 2, HALF, COL), BF),
        pltpu.VMEM((2, 2, ROWS, COL), BF),
        dma((6,)),
        dma((11,)),
        dma((3, 4)),
        dma((3, 3)),
        dma((3,)),
        dma((3, 2)),
        dma((3, 2)),
        dma((3, 2)),
        dma((3, 2)),
        dma((2, 2)),
        dma((2, 2)),
        dma((2, 2, 7)),
        dma((2,)),
        dma((2, 2, 7)),
        dma((2,)),
    ]
    hbm = pl.BlockSpec(memory_space=pltpu.HBM)
    vmem = pl.BlockSpec(memory_space=pltpu.VMEM)
    out, wgrad = pl.pallas_call(
        kernel,
        out_shape=(
            pltpu.VMEM((2, TOK, FEAT), BF),
            pltpu.VMEM((3, 2, HID, FEAT), BF),
        ),
        in_specs=[hbm] * 6,
        out_specs=(vmem, vmem),
        scratch_shapes=scratch,
        compiler_params=pltpu.CompilerParams(
            collective_id=0, has_side_effects=True, vmem_limit_bytes=50 * 1024 * 1024
        ),
    )(
        labels.reshape(1, TOK),
        tokens,
        grad_out,
        jnp.swapaxes(w_gate, 1, 2),
        jnp.swapaxes(w_up, 1, 2),
        w_down,
    )
    out = pltpu.with_memory_space_constraint(out, pltpu.VMEM)
    wgrad = pltpu.with_memory_space_constraint(wgrad, pltpu.VMEM)
    weights = jax.ShapeDtypeStruct((2, HID, FEAT), BF)
    acts = jax.ShapeDtypeStruct((TOK, FEAT), BF)
    mixed, grad_tokens, gate_t, up_t, down = pl.pallas_call(
        writer,
        out_shape=(acts, acts, weights, weights, weights),
        in_specs=[vmem, vmem],
        out_specs=(hbm,) * 5,
        scratch_shapes=[dma((8,))],
        compiler_params=pltpu.CompilerParams(vmem_limit_bytes=4 * 1024 * 1024),
    )(out, wgrad)
    return mixed, grad_tokens, jnp.swapaxes(gate_t, 1, 2), jnp.swapaxes(up_t, 1, 2), down


def solution(mesh):
    in_specs = (
        P("expert", "dp"),
        P("expert", None),
        P("expert", "dp"),
        P("expert", "dp", "tensor"),
        P("expert", "dp", "tensor"),
        P("expert", "tensor", "dp"),
    )
    out_specs = (
        P("expert", "dp"),
        P("expert", "dp"),
        P("expert", "dp", "tensor"),
        P("expert", "dp", "tensor"),
        P("expert", "tensor", "dp"),
    )
    return jax.shard_map(body, mesh=mesh, in_specs=in_specs, out_specs=out_specs, check_vma=False)
```
